256 devices in a mesh: depth: 8 (over y, core), rays: 32 (over z, x).
Axes of the slice: x: 4, y: 4, z: 8, core: 2. Of those that a mesh axis runs over, the one named last changes fastest.
Arguments:
- encodings: bfloat16 [8, 163840, 8, 128], P('depth', 'rays'), may hold values from -6 to 6
- spacing: float32 [8, 8, 163840], P('depth', None, 'rays'), may hold values from 0.01 to 0.1
- ray_ids: int32 [8, 163840], P('depth', 'rays'), may hold values from 0 to 8191, as said below
- live_count: int32 [8, 32], P('depth', 'rays'), may hold values from 1280 to 5120, as said below
- pixel_of_ray: int32 [262144], P('rays'), may hold values from 0 to 262143, as said below
- w_first: bfloat16 [8, 128, 128], P('depth'), may hold values from -0.5 to 0.5
- b_first: float32 [8, 128], P('depth'), may hold values from -3 to 3
- w_second: bfloat16 [8, 128, 128], P('depth'), may hold values from -0.5 to 0.5
- b_second: float32 [8, 128], P('depth'), may hold values from -3 to 3
- w_density: bfloat16 [8, 128], P('depth'), may hold values from -0.5 to 0.5
- w_feature: bfloat16 [8, 128, 128], P('depth'), may hold values from -1.5 to 1.5
- kernel_one: bfloat16 [5, 5, 128, 128], replicated, may hold values from -0.109375 to 0.109375
- bias_one: float32 [128], replicated, may hold values from -2 to 2
- kernel_two: bfloat16 [5, 5, 128, 128], replicated, may hold values from -0.109375 to 0.109375
- bias_two: float32 [128], replicated, may hold values from -2 to 2
Outputs:
- rendered: bfloat16 [512, 512, 128], P('rays', 'depth')
The draws below stay inside these ranges and needn't reach their ends.
Inputs may be any that keep to these rules, and one draw needn't show every extreme that they name: `ray_ids`: within the 5120 slots of one partition and bundle the ray ids are distinct; only the first live_count slots are live. `live_count`: some partition and bundle has all 5120 slots live. `pixel_of_ray`: A permutation of the image's pixels. Split the image into blocks of 16 rows by 64 columns: every bundle's 8192 rays hold exactly 32 pixels of every block.
All inputs are finite; a program needn't handle non-finite values.
Results may differ from the reference program's by a relative error of at most 0.013.
Values may be sent and summed in bfloat16 or wider, within the bound.
No kernel may reach another device: no remote copies, remote signals or barrier semaphores. Data moves between devices by JAX's collectives and lax.ppermute only.
A program may use at most 128 MiB of HBM per device.

```python
import math
import jax
import jax.numpy as jnp
from jax import lax

ENC = 128
WIDTH = 128
FEAT = 128
SAMPLES = 8
KSIZE = 5
TH = 16
TW = 64
DEPTHS = 8
BUNDLES = 32
RAYS_DEV = 8192
SEG_BLK = 5120
HEIGHT = 512
WIDE = 512


def draw_ray_ids(key, part):
    key_list = jax.random.split(jax.random.fold_in(key, 11), DEPTHS * BUNDLES)
    shuffled = jax.vmap(lambda one_key: jax.random.permutation(one_key, RAYS_DEV))(key_list)
    return shuffled[:, :SEG_BLK].reshape(DEPTHS, BUNDLES * SEG_BLK).astype(jnp.int32)


def draw_live_count(key, part):
    key_draw, key_pick = jax.random.split(jax.random.fold_in(key, 23))
    counts = jax.random.randint(key_draw, (DEPTHS * BUNDLES,), SEG_BLK // 4, SEG_BLK + 1)
    chosen = jax.random.randint(key_pick, (), 0, DEPTHS * BUNDLES)
    counts = counts.at[chosen].set(SEG_BLK)
    return counts.reshape(DEPTHS, BUNDLES).astype(jnp.int32)


def draw_pixel_of_ray(key, part):
    key_block, key_order = jax.random.split(jax.random.fold_in(key, 37))
    blocks = BUNDLES * DEPTHS
    per_block = TH * TW // BUNDLES
    inside = jax.vmap(lambda one_key: jax.random.permutation(one_key, TH * TW))(jax.random.split(key_block, blocks))
    inside = inside.reshape(blocks, BUNDLES, per_block).transpose(1, 0, 2)
    block_ids = jnp.arange(blocks, dtype=jnp.int32)
    tile_row = block_ids // DEPTHS
    col_block = block_ids % DEPTHS
    pixel_row = tile_row[None, :, None] * TH + inside // TW
    pixel_col = col_block[None, :, None] * TW + inside % TW
    pixels = (pixel_row * (TW * DEPTHS) + pixel_col).reshape(BUNDLES, RAYS_DEV)
    shuffles = jax.vmap(lambda one_key: jax.random.permutation(one_key, RAYS_DEV))(jax.random.split(key_order, BUNDLES))
    pixels = jnp.take_along_axis(pixels, shuffles, axis=1)
    return pixels.reshape(BUNDLES * RAYS_DEV).astype(jnp.int32)


def shard_levels(rng, extent, cuts, smallest, high):
    def one(position, shards_of):
        heights = jax.random.uniform(jax.random.fold_in(jax.random.fold_in(rng, 6), position), (shards_of,), jnp.float32, smallest / len(cuts), high / len(cuts))
        return jnp.repeat(jnp.exp(heights), extent[position] // shards_of).reshape((-1,) + (1,) * (len(extent) - position - 1))

    level = one(*cuts[0])
    for cut in cuts[1:]:
        level = level * one(*cut)
    return level


def bell_draw(own_key, shape, spread, bound, cuts=(), held_as=jnp.bfloat16):
    drawn = spread * jax.random.normal(own_key, shape, jnp.float32)
    if cuts:
        drawn = drawn * shard_levels(own_key, shape, cuts, -0.22, 0.18)
    return jnp.clip(drawn, -bound, bound).astype(held_as)


def setup_inputs(seed: int = 0) -> dict:
    arg_keys = jax.random.split(jax.random.key(seed), 16)
    return {
        "encodings": bell_draw(arg_keys[0], (DEPTHS, BUNDLES * SEG_BLK, SAMPLES, ENC), 1.0, 6.0, ((0, 8), (1, 32))),
        "spacing": jnp.clip(jnp.exp(math.log(0.1) - 2.3025851 * jax.random.uniform(arg_keys[1], (DEPTHS, SAMPLES, BUNDLES * SEG_BLK), jnp.float32) ** shard_levels(arg_keys[1], (DEPTHS, SAMPLES, BUNDLES * SEG_BLK), ((0, 8), (2, 32)), -0.2, 0.2)), 0.01, 0.1),
        "ray_ids": draw_ray_ids(jax.random.fold_in(arg_keys[15], 71), 0),
        "live_count": draw_live_count(jax.random.fold_in(arg_keys[15], 71), 0),
        "pixel_of_ray": draw_pixel_of_ray(jax.random.fold_in(arg_keys[15], 71), 0),
        "w_first": bell_draw(arg_keys[5], (DEPTHS, ENC, WIDTH), ENC ** -0.5, 0.5, ((0, 8),)),
        "b_first": bell_draw(arg_keys[6], (DEPTHS, WIDTH), 0.5, 3.0, ((0, 8),), jnp.float32),
        "w_second": bell_draw(arg_keys[7], (DEPTHS, WIDTH, WIDTH), WIDTH ** -0.5, 0.5, ((0, 8),)),
        "b_second": bell_draw(arg_keys[8], (DEPTHS, WIDTH), 0.5, 3.0, ((0, 8),), jnp.float32),
        "w_density": bell_draw(arg_keys[9], (DEPTHS, WIDTH), WIDTH ** -0.5, 0.5, ((0, 8),)),
        "w_feature": bell_draw(arg_keys[10], (DEPTHS, WIDTH, FEAT), (WIDTH // 8) ** -0.5, 1.5, ((0, 8),)),
        "kernel_one": bell_draw(arg_keys[11], (KSIZE, KSIZE, FEAT, FEAT), (KSIZE * KSIZE * FEAT) ** -0.5, 0.109375),
        "bias_one": bell_draw(arg_keys[12], (FEAT,), 0.3, 2.0, (), jnp.float32),
        "kernel_two": bell_draw(arg_keys[13], (KSIZE, KSIZE, FEAT, FEAT), (KSIZE * KSIZE * FEAT) ** -0.5, 0.109375),
        "bias_two": bell_draw(arg_keys[14], (FEAT,), 0.3, 2.0, (), jnp.float32),
    }


def slot_terms(encoded, spacing_block, live_total, w_first, b_first, w_second, b_second, w_density, w_feature):
    slot_total, samples, enc_width = encoded.shape
    flat_rows = encoded.reshape(slot_total * samples, enc_width)
    hidden_one = jnp.maximum(jnp.dot(flat_rows, w_first, preferred_element_type=jnp.float32) + b_first, 0.0).astype(jnp.bfloat16)
    hidden_two = jnp.maximum(jnp.dot(hidden_one, w_second, preferred_element_type=jnp.float32) + b_second, 0.0).astype(jnp.bfloat16)
    density = jax.nn.softplus(jnp.dot(hidden_two, w_density, preferred_element_type=jnp.float32)).reshape(slot_total, samples)
    feature = jnp.dot(hidden_two, w_feature, preferred_element_type=jnp.float32).reshape(slot_total, samples, -1)
    opacity = density * spacing_block
    within = jnp.cumsum(opacity, axis=1) - opacity
    weight = jnp.exp(-within) * (1.0 - jnp.exp(-opacity))
    colour = jnp.einsum("ns,nsf->nf", weight, feature)
    live_mask = (jnp.arange(slot_total) < live_total).astype(jnp.float32)
    return colour * live_mask[:, None], jnp.sum(opacity, axis=1) * live_mask


def convolve(image, kernel):
    return lax.conv_general_dilated(image.astype(jnp.float32)[None], kernel.astype(jnp.float32), (1, 1), "SAME", dimension_numbers=("NHWC", "HWIO", "NHWC"), precision=lax.Precision.HIGHEST)[0]


def reference(encodings, spacing, ray_ids, live_count, pixel_of_ray, w_first, b_first, w_second, b_second, w_density, w_feature, kernel_one, bias_one, kernel_two, bias_two):
    enc_all = encodings.reshape(DEPTHS, BUNDLES, SEG_BLK, SAMPLES, ENC)
    gaps_all = spacing.reshape(DEPTHS, SAMPLES, BUNDLES, SEG_BLK).transpose(0, 2, 3, 1)
    ids_all = ray_ids.reshape(DEPTHS, BUNDLES, SEG_BLK)

    def one_depth(carry, inputs):
        before, total = carry
        enc_depth, gaps_depth, ids_depth, count_depth, wa_depth, ba_depth, wb_depth, bb_depth, wd_depth, wf_depth = inputs

        def one_bundle(item):
            enc_bundle, gaps_bundle, ids_bundle, count_bundle = item
            colour, depth_sum = slot_terms(enc_bundle, gaps_bundle, count_bundle, wa_depth, ba_depth, wb_depth, bb_depth, wd_depth, wf_depth)
            ray_colour = jnp.zeros((RAYS_DEV, FEAT), jnp.float32).at[ids_bundle].add(colour)
            ray_depth = jnp.zeros((RAYS_DEV,), jnp.float32).at[ids_bundle].add(depth_sum)
            return ray_colour, ray_depth

        ray_colour, ray_depth = lax.map(one_bundle, (enc_depth, gaps_depth, ids_depth, count_depth))
        partial_value = (jnp.exp(-before)[..., None] * ray_colour).astype(jnp.bfloat16)
        return (before + ray_depth, total + partial_value.astype(jnp.float32)), None

    start = (jnp.zeros((BUNDLES, RAYS_DEV), jnp.float32), jnp.zeros((BUNDLES, RAYS_DEV, FEAT), jnp.float32))
    final_state, unused = lax.scan(one_depth, start, (enc_all, gaps_all, ids_all, live_count, w_first, b_first, w_second, b_second, w_density, w_feature))
    composite = final_state[1].astype(jnp.bfloat16).reshape(BUNDLES * RAYS_DEV, FEAT)
    image = jnp.zeros((HEIGHT * WIDE, FEAT), jnp.bfloat16).at[pixel_of_ray].set(composite).reshape(HEIGHT, WIDE, FEAT)
    hidden_image = jnp.maximum(convolve(image, kernel_one) + bias_one, 0.0).astype(jnp.bfloat16)
    return (convolve(hidden_image, kernel_two) + bias_two).astype(jnp.bfloat16)
```

```python
import functools

import jax
import jax.numpy as jnp
from jax import lax
from jax.experimental import pallas as pl
from jax.experimental.pallas import tpu as pltpu
from jax.sharding import PartitionSpec as P

FEAT = 128
SAMPLES = 8
TH = 16
TW = 64
WIDE = 512
HEIGHT = 512
SLOTS = 5120
RAYS = 8192
LANES = 128
BLOCKS = 256
HALO = 4
PITCH = TW + 16
PIECE = 1024
PACK = PIECE + 16
SUPER = 256
f32 = jnp.float32
bf16 = jnp.bfloat16
i32 = jnp.int32


def dot_nt(lhs, rhs):
    return lax.dot_general(lhs, rhs, (((1,), (1,)), ((), ())), preferred_element_type=f32)


def dot_nn(lhs, rhs):
    return jnp.dot(lhs, rhs, preferred_element_type=f32)


def iota(shape, axis):
    return lax.broadcasted_iota(i32, shape, axis)


def as_bf16(mask):
    return jnp.where(mask, 1.0, 0.0).astype(bf16)


def index_kernel(where_ref, pixel_ref, ids_ref, pos_ref, info_ref, hi_scr, lo_scr):
    my_core, my_y, bundle = where_ref[0], where_ref[1], where_ref[2]
    pixel = pixel_ref[...]
    row, col = pixel >> 9, pixel & (WIDE - 1)
    block_col = col >> 6
    core_rel = (block_col & 1) ^ my_core
    y_rel = ((block_col >> 1) - my_y) & 3
    group = core_rel * 128 + y_rel * 32 + (row >> 4)
    local_row, local_col = (row & (TH - 1)).astype(f32), (col & (TW - 1)).astype(f32)
    upper = as_bf16(iota((LANES, 2 * LANES), 0) < iota((LANES, 2 * LANES), 1))
    group_iota = iota((BLOCKS, LANES), 0)
    carry = jnp.zeros((BLOCKS, LANES), f32)
    own = jnp.zeros((8, 2 * LANES), f32)
    lane_iota = iota((LANES, LANES), 0)
    for j in range(RAYS // LANES):
        g = group[j : j + 1, :]
        hit = group_iota == g
        member = jnp.where(hit, 1.0, 0.0)
        counts = dot_nn(member.astype(bf16), upper)
        rank = jnp.sum(member * (counts[:, :LANES] + carry), axis=0, keepdims=True)
        carry = carry + counts[:, LANES:]
        hi = g >> 2
        lo = (g & 3) * 32 + rank.astype(i32)
        hi_scr[j : j + 1, :] = hi.astype(f32)
        lo_scr[j : j + 1, :] = lo.astype(f32)
        mine = as_bf16(iota((8, LANES), 0) == hi)
        at = lane_iota == lo
        wanted = jnp.concatenate(
            [
                jnp.where(at, local_row[j : j + 1, :], 0.0).astype(bf16),
                jnp.where(at, local_col[j : j + 1, :], 0.0).astype(bf16),
            ],
            axis=0,
        )
        own = own + dot_nt(mine, wanted)
    own_row, own_col = own[:, :LANES], own[:, LANES:]
    lane8 = iota((8, LANES), 1)
    quarter = bundle & 3
    for q in range(4):
        shift = ((quarter - q) & 3) * 32
        keep = (lane8 >> 5) == quarter
        info_ref[q, 0] = jnp.where(keep, pltpu.roll(own_row, shift, 1), 0.0)
        info_ref[q, 1] = jnp.where(keep, pltpu.roll(own_col, shift, 1), 0.0)
    table = jnp.concatenate([hi_scr[...], lo_scr[...]], axis=1).astype(bf16)
    high_iota = iota((RAYS // LANES, LANES), 0)
    for j in range(SLOTS // LANES):
        ids = ids_ref[j : j + 1, :]
        high = as_bf16(high_iota == (ids >> 7))
        found = lax.dot_general(table, high, (((0,), (0,)), ((), ())), preferred_element_type=f32)
        low = lane_iota == (ids & (LANES - 1))
        hi = jnp.sum(jnp.where(low, found[:LANES], 0.0), axis=0, keepdims=True)
        lo = jnp.sum(jnp.where(low, found[LANES:], 0.0), axis=0, keepdims=True)
        pos_ref[j : j + 1, :] = hi.astype(i32) * LANES + lo.astype(i32)


def segment_kernel(
    pos_smem,
    live_smem,
    enc_ref,
    gap_ref,
    pos_ref,
    w1_ref,
    b1_ref,
    w2_ref,
    b2_ref,
    wd_ref,
    wf_ref,
    near_ref,
    far_ref,
    spread,
    colour,
    depth,
):
    step = pl.program_id(0)
    per_step = enc_ref.shape[0] // (SUPER * SAMPLES)
    live = live_smem[0]

    @pl.when(step == 0)
    def _():
        spread[...] = jnp.zeros_like(spread)

    lane = iota((8, SUPER), 1)
    row8 = iota((8, SUPER), 0)
    sample = lane & 7
    of_slot = iota((32, SUPER), 0) == (iota((32, SUPER), 1) >> 3)
    pick = jnp.concatenate(
        [
            as_bf16(
                iota((SUPER, LANES), 0) == (iota((SUPER, LANES), 1) - 32 * q) * 8 + 7
            )
            for q in range(4)
        ],
        axis=1,
    )
    half = SUPER * SAMPLES // 2
    for part in range(per_step):
        base = part * SUPER * SAMPLES
        x = jnp.concatenate(
            [enc_ref[base : base + half, :], enc_ref[base + half : base + 2 * half, :]], axis=1
        )
        h1 = jnp.maximum(dot_nn(x, w1_ref[...]) + b1_ref[...], 0.0).astype(bf16)
        h2 = jnp.maximum(dot_nn(h1, w2_ref[...]) + b2_ref[...], 0.0).astype(bf16)
        pre = jnp.zeros((8, SUPER), f32)
        for i in range(4):
            pre = pre + dot_nt(wd_ref[i], h2[i * SUPER : (i + 1) * SUPER, :])
        soft = jnp.maximum(pre, 0.0) + jnp.log1p(jnp.exp(-jnp.abs(pre)))
        opacity = soft * gap_ref[part * 8 : part * 8 + 8, :]
        inc = opacity
        for shift in (1, 2, 4):
            inc = inc + jnp.where(sample >= shift, pltpu.roll(inc, shift, 1), 0.0)
        weight = jnp.exp(opacity - inc) * (1.0 - jnp.exp(-opacity))
        slot = (step * per_step + part) * SUPER + row8 * 32 + (lane >> 3)
        alive = slot < live
        weight = jnp.where(alive, weight, 0.0)
        inc = jnp.where(alive, inc, 0.0)
        inc_hi = inc.astype(bf16)
        inc_lo = (inc - inc_hi.astype(f32)).astype(bf16)
        picked = dot_nn(inc_hi, pick) + dot_nn(inc_lo, pick)
        lined = jnp.zeros((8, LANES), f32)
        r8 = iota((8, LANES), 0)
        for q in range(4):
            lined = lined + jnp.where((r8 & 3) == q, picked[:, q * LANES : (q + 1) * LANES], 0.0)
        block = (step * per_step + part) * 2
        depth[pl.ds(block, 1), :] = jnp.sum(lined[:4], axis=0, keepdims=True)
        depth[pl.ds(block + 1, 1), :] = jnp.sum(lined[4:], axis=0, keepdims=True)
        gathered = [None] * 8
        for i in range(4):
            left = jnp.where(of_slot, weight[i : i + 1, :], 0.0)
            right = jnp.where(of_slot, weight[i + 4 : i + 5, :], 0.0)
            both = jnp.concatenate([left, right], axis=0).astype(bf16)
            summed = dot_nn(both, h2[i * SUPER : (i + 1) * SUPER, :])
            gathered[i] = summed[:32, :LANES]
            gathered[i + 4] = summed[32:, LANES:]
        mixed = jnp.concatenate(gathered, axis=0).astype(bf16)
        colour[...] = dot_nn(mixed, wf_ref[...])
        first = (step * per_step + part) * SUPER
        for s in range(SUPER):
            spread[pl.ds(pos_smem[first + s], 1), :] = colour[s : s + 1, :]

    @pl.when(step == pl.num_programs(0) - 1)
    def _():
        table = jnp.zeros((RAYS // LANES, 2 * LANES), f32)
        for j in range(SLOTS // LANES):
            at = pos_ref[j : j + 1, :]
            here = depth[j : j + 1, :]
            high = as_bf16(iota((RAYS // LANES, LANES), 0) == (at >> 7))
            low = iota((LANES, LANES), 0) == (at & (LANES - 1))
            coarse = here.astype(bf16).astype(f32)
            wanted = jnp.concatenate(
                [
                    jnp.where(low, coarse, 0.0).astype(bf16),
                    jnp.where(low, here - coarse, 0.0).astype(bf16),
                ],
                axis=0,
            )
            table = table + dot_nt(high, wanted)
        for g in range(4):
            for k, out in enumerate((near_ref, far_ref)):
                at = (4 * k + g) * PIECE
                out[g, :PIECE, :] = spread[at : at + PIECE, :].astype(bf16)
                rows = slice((4 * k + g) * 8, (4 * k + g) * 8 + 8)
                out[g, PIECE:, :] = jnp.concatenate(
                    [table[rows, :LANES], table[rows, LANES:]], axis=0
                ).astype(bf16)


def read_depth(ref):
    rows = ref[PIECE:, :].astype(f32)
    return rows[:8] + rows[8:]


def scaled(ref, factors, i):
    return ref[i * LANES : (i + 1) * LANES, :].astype(f32) * factors[:, i : i + 1]


def pair_kernel(where_ref, near_ref, arrived_ref, *outs):
    first = where_ref[0] == 0
    for g in range(4):
        mine, other = near_ref.at[g], arrived_ref.at[g]
        d_mine, d_other = read_depth(mine), read_depth(other)
        fade = jnp.exp(-jnp.where(first, d_mine, d_other))
        one = jnp.ones_like(fade)
        f_mine = jnp.where(first, one, fade).T
        f_other = jnp.where(first, fade, one).T
        for i in range(8):
            outs[g][i * LANES : (i + 1) * LANES, :] = (
                scaled(mine, f_mine, i) + scaled(other, f_other, i)
            ).astype(bf16)
        both = d_mine + d_other
        coarse = both.astype(bf16).astype(f32)
        outs[g][PIECE:, :] = jnp.concatenate([coarse, both - coarse], axis=0).astype(bf16)


def merge_kernel(where_ref, p0_ref, p1_ref, p2_ref, p3_ref, info_ref, out_ref):
    y = where_ref[1]
    pieces = (p0_ref, p1_ref, p2_ref, p3_ref)
    places = [(y - k) & 3 for k in range(4)]
    depths = [read_depth(ref) for ref in pieces]
    factors = []
    for a in range(4):
        before = jnp.zeros_like(depths[0])
        for b in range(4):
            if b != a:
                before = before + jnp.where(places[b] < places[a], depths[b], 0.0)
        factors.append(jnp.exp(-before).T)
    for i in range(8):
        total = scaled(pieces[0], factors[0], i)
        for k in range(1, 4):
            total = total + scaled(pieces[k], factors[k], i)
        total = total.astype(bf16)
        for q in range(4):
            tile = i * 4 + q
            out_ref[tile, :32, :] = total[q * 32 : q * 32 + 32, :]
            extra = jnp.concatenate(
                [
                    info_ref[q, 0, i : i + 1, :],
                    info_ref[q, 1, i : i + 1, :],
                    jnp.zeros((6, LANES), f32),
                ],
                axis=0,
            )
            out_ref[tile, 32:, :] = extra.astype(bf16)


def place_kernel(in_ref, out_ref):
    total = jnp.zeros((TH * TW, FEAT), f32)
    pixel_iota = iota((TH * TW, LANES), 0)
    for g in range(8):
        rows = jnp.concatenate([in_ref[4 * g + q, :32, :] for q in range(4)], axis=0)
        place = in_ref[4 * g, 32:, :].astype(f32)
        for q in range(1, 4):
            place = place + in_ref[4 * g + q, 32:, :].astype(f32)
        pixel = (place[0:1, :] * TW + place[1:2, :]).astype(i32)
        total = total + dot_nn(as_bf16(pixel_iota == pixel), rows)
    out_ref[...] = total.astype(bf16)


def whole(shape):
    return pl.BlockSpec(shape, lambda *_: (0,) * len(shape))


def shape_of(shape, dtype):
    return jax.ShapeDtypeStruct(shape, dtype)


VMEM = pl.BlockSpec(memory_space=pltpu.VMEM)
SMEM = pl.BlockSpec(memory_space=pltpu.SMEM)


def segments(pos, live, enc, gaps, w1, b1, w2, b2, wd, wf, per_step=2):
    def twice(w):
        zero = jnp.zeros_like(w)
        return jnp.concatenate(
            [jnp.concatenate([w, zero], axis=1), jnp.concatenate([zero, w], axis=1)], axis=0
        )

    eye = jnp.eye(8, dtype=bf16)
    heads = jnp.stack(
        [
            jnp.concatenate([eye[i][:, None] * wd[None], eye[i + 4][:, None] * wd[None]], axis=1)
            for i in range(4)
        ]
    )
    rows = per_step * SUPER * SAMPLES
    steps = SLOTS * SAMPLES // rows
    out = shape_of((4, PACK, FEAT), bf16)
    return pl.pallas_call(
        segment_kernel,
        grid_spec=pltpu.PrefetchScalarGridSpec(
            num_scalar_prefetch=2,
            grid=(steps,),
            in_specs=[
                pl.BlockSpec((rows, FEAT), lambda i, *_: (i, 0)),
                pl.BlockSpec((per_step * 8, SUPER), lambda i, *_: (i, 0)),
                whole((SLOTS // LANES, LANES)),
                whole((256, 256)),
                whole((1, 256)),
                whole((256, 256)),
                whole((1, 256)),
                whole((4, 8, 256)),
                whole((128, 128)),
            ],
            out_specs=[whole((4, PACK, FEAT))] * 2,
            scratch_shapes=[
                pltpu.VMEM((RAYS, FEAT), f32),
                pltpu.VMEM((SUPER, FEAT), f32),
                pltpu.VMEM((SLOTS // LANES, LANES), f32),
            ],
        ),
        out_shape=[out, out],
        name="segments",
    )(
        pos.reshape(SLOTS),
        live,
        enc,
        gaps,
        pos,
        twice(w1),
        jnp.tile(b1, 2)[None],
        twice(w2),
        jnp.tile(b2, 2)[None],
        heads,
        wf,
    )


def exchanged(low, high, axis):
    size = lax.axis_size(axis)
    up = [(i, i + 1) for i in range(size - 1)]
    down = [(j, i) for i, j in up]
    return lax.ppermute(high, axis, up), lax.ppermute(low, axis, down)


def shift_columns(source, shifted, rows, first):
    for j in range(5):
        shifted[:rows, j * LANES : (j + 1) * LANES] = source[first + j : first + j + rows, :].astype(
            bf16
        )


def conv_kernel(
    where_ref, mid_ref, top_ref, low_ref, k1_ref, b1_ref, k2_ref, b2_ref, out_ref, rows, shifted
):
    place, tile = where_ref[1] * 2 + where_ref[0], where_ref[2]
    rows[: 4 * PITCH, :] = top_ref[...].astype(f32)
    rows[4 * PITCH : 20 * PITCH, :] = mid_ref[...].astype(f32)
    rows[20 * PITCH : 24 * PITCH, :] = low_ref[...].astype(f32)
    rows[24 * PITCH :, :] = jnp.zeros((16, FEAT), f32)
    shift_columns(rows, shifted, 24 * PITCH, 4)
    flat = iota((4 * PITCH, FEAT), 0)
    y_in, x = flat // PITCH, flat % PITCH
    col = place * TW - 2 + x
    for part in range(5):
        base = part * 4 * PITCH
        total = jnp.zeros((4 * PITCH, FEAT), f32) + b1_ref[...]
        for i in range(5):
            at = base + i * PITCH
            total = total + dot_nn(shifted[at : at + 4 * PITCH, :], k1_ref[i])
        row = tile * TH - 2 + part * 4 + y_in
        inside = (row >= 0) & (row < HEIGHT) & (col >= 0) & (col < WIDE)
        rows[base : base + 4 * PITCH, :] = jnp.where(inside, jnp.maximum(total, 0.0), 0.0)
    shift_columns(rows, shifted, 20 * PITCH, 0)
    for part in range(4):
        base = part * 4 * PITCH
        total = jnp.zeros((4 * PITCH, FEAT), f32) + b2_ref[...]
        for i in range(5):
            at = base + i * PITCH
            total = total + dot_nn(shifted[at : at + 4 * PITCH, :], k2_ref[i])
        total = total.astype(bf16)
        for y in range(4):
            out_ref[part * 4 + y] = total[y * PITCH : y * PITCH + TW, :]


def index_call(where, pixel, ids):
    return pl.pallas_call(
        index_kernel,
        in_specs=[SMEM, VMEM, VMEM],
        out_specs=[VMEM, VMEM],
        out_shape=[shape_of((SLOTS // LANES, LANES), i32), shape_of((4, 2, 8, LANES), f32)],
        scratch_shapes=[pltpu.VMEM((RAYS // LANES, LANES), f32)] * 2,
        name="index",
    )(where, pixel.reshape(RAYS // LANES, LANES), ids.reshape(SLOTS // LANES, LANES))


def on_device(
    encodings,
    spacing,
    ray_ids,
    live_count,
    pixel_of_ray,
    w_first,
    b_first,
    w_second,
    b_second,
    w_density,
    w_feature,
    kernel_one,
    bias_one,
    kernel_two,
    bias_two,
):
    place = lax.axis_index("depth")
    tile = lax.axis_index("rays")
    where = jnp.stack([place & 1, place >> 1, tile]).astype(i32)
    pos, info = index_call(where, pixel_of_ray, ray_ids)
    gaps = spacing[0].T.reshape(SLOTS // 32, SUPER)
    near, far = segments(
        pos,
        live_count.reshape(1),
        encodings.reshape(SLOTS * SAMPLES, FEAT),
        gaps,
        w_first[0],
        b_first[0],
        w_second[0],
        b_second[0],
        w_density[0],
        w_feature[0],
    )
    arrived = lax.ppermute(far, "depth", [(i, i ^ 1) for i in range(8)])
    piece = shape_of((PACK, FEAT), bf16)
    pieces = pl.pallas_call(
        pair_kernel,
        in_specs=[SMEM, VMEM, VMEM],
        out_specs=[VMEM] * 4,
        out_shape=[piece] * 4,
        name="pair",
    )(where, near, arrived)
    got = [
        lax.ppermute(pieces[k], "depth", [(i, (i + 2 * k) % 8) for i in range(8)])
        for k in range(1, 4)
    ]
    outgoing = pl.pallas_call(
        merge_kernel,
        in_specs=[SMEM] + [VMEM] * 5,
        out_specs=VMEM,
        out_shape=shape_of((32, 40, FEAT), bf16),
        name="merge",
    )(where, pieces[0], *got, info)
    incoming = lax.all_to_all(outgoing, "rays", split_axis=0, concat_axis=0, tiled=True)
    image = pl.pallas_call(
        place_kernel,
        in_specs=[VMEM],
        out_specs=VMEM,
        out_shape=shape_of((TH * TW, FEAT), bf16),
        name="place",
    )(incoming)
    block = image.reshape(TH, TW, FEAT)
    before, after = exchanged(block[:, :8], block[:, TW - 8 :], "depth")
    middle = jnp.concatenate([before, block, after], axis=1)
    top, low = exchanged(middle[:HALO], middle[TH - HALO :], "rays")
    return pl.pallas_call(
        conv_kernel,
        in_specs=[SMEM] + [VMEM] * 7,
        out_specs=VMEM,
        out_shape=shape_of((TH, TW, FEAT), bf16),
        scratch_shapes=[
            pltpu.VMEM((24 * PITCH + 16, FEAT), f32),
            pltpu.VMEM((24 * PITCH, 5 * FEAT), bf16),
        ],
        name="conv",
    )(
        where,
        middle.reshape(TH * PITCH, FEAT),
        top.reshape(HALO * PITCH, FEAT),
        low.reshape(HALO * PITCH, FEAT),
        kernel_one.reshape(5, 5 * FEAT, FEAT),
        bias_one[None],
        kernel_two.reshape(5, 5 * FEAT, FEAT),
        bias_two[None],
    )


def solution(mesh):
    in_specs = (
        P("depth", "rays", None, None),
        P("depth", None, "rays"),
        P("depth", "rays"),
        P("depth", "rays"),
        P("rays"),
        P("depth", None, None),
        P("depth", None),
        P("depth", None, None),
        P("depth", None),
        P("depth", None),
        P("depth", None, None),
        P(),
        P(),
        P(),
        P(),
    )
    return jax.shard_map(
        on_device, mesh=mesh, in_specs=in_specs, out_specs=P("rays", "depth", None), check_vma=False
    )
```

```python
import functools

import jax
import jax.numpy as jnp
from jax import lax
from jax.experimental import pallas as pl
from jax.experimental.pallas import tpu as pltpu
from jax.sharding import PartitionSpec as P

FEAT = 128
SAMPLES = 8
TH = 16
TW = 64
WIDE = 512
HEIGHT = 512
SLOTS = 5120
RAYS = 8192
LANES = 128
HALO = 4
PITCH = TW + 16
PAIR_ORDER = (2, 1, 3, 0)
PIECE = 1024
PACK = PIECE + 16
SUPER = 256
f32 = jnp.float32
bf16 = jnp.bfloat16
i32 = jnp.int32


def dot_nt(lhs, rhs):
    return lax.dot_general(lhs, rhs, (((1,), (1,)), ((), ())), preferred_element_type=f32)


def dot_nn(lhs, rhs):
    return jnp.dot(lhs, rhs, preferred_element_type=f32)


def iota(shape, axis):
    return lax.broadcasted_iota(i32, shape, axis)


def as_bf16(mask):
    return jnp.where(mask, 1.0, 0.0).astype(bf16)


def coordinates():
    place = lax.axis_index("depth")
    return place & 1, place >> 1, lax.axis_index("rays")


def rank_sum(parts):
    total = parts[0]
    for part in parts[1:]:
        total = total + part
    return jnp.sum(total, axis=0, keepdims=True)


def index_rays(pixel_ref, ids_ref, pos_ref, ray_ref):
    my_core, my_y, _ = coordinates()
    pixel = pixel_ref[...]
    row, col = pixel >> 9, pixel & (WIDE - 1)
    block_col = col >> 6
    core_rel = (block_col & 1) ^ my_core
    y_rel = ((block_col >> 1) - my_y) & 3
    group = core_rel * 128 + y_rel * 32 + (row >> 4)
    column = group.astype(f32).T.astype(i32)
    earlier = iota((LANES, LANES), 0) < iota((LANES, LANES), 1)
    iota16 = iota((16, LANES), 0)
    seen = jnp.zeros((16, 16), f32)
    ranks = []
    for j in range(RAYS // LANES):
        g = group[j : j + 1, :]
        same = jnp.where((column[:, j : j + 1] == g) & earlier, 1.0, 0.0)
        coarse = as_bf16(iota16 == (g >> 4))
        fine = iota16 == (g & 15)
        found = jnp.where(fine, dot_nn(seen.astype(bf16), coarse), 0.0)
        seen = seen + dot_nt(as_bf16(fine), coarse)
        parts = [same[8 * k : 8 * k + 8] for k in range(16)] + [found[:8], found[8:]]
        ranks.append(rank_sum(parts))
    rank = jnp.concatenate(ranks, axis=0).astype(i32)
    high = group >> 2
    low = (group & 3) * 32 + rank
    ray_ref[...] = high * LANES + low
    table = jnp.concatenate(
        [(high * LANES).astype(f32).T, low.astype(f32).T], axis=1
    ).astype(bf16)
    high_iota = iota((RAYS // LANES, LANES), 0)
    lane_iota = iota((LANES, LANES), 0)
    for j in range(SLOTS // LANES):
        ids = ids_ref[j : j + 1, :]
        hot = as_bf16(high_iota == (ids >> 7))
        found = dot_nn(table, jnp.concatenate([hot, hot], axis=0))
        found = jnp.where(lane_iota == (ids & (LANES - 1)), found, 0.0)
        pos_ref[j : j + 1, :] = rank_sum([found[8 * k : 8 * k + 8] for k in range(16)]).astype(i32)


def arrange_taps(k1_ref, k2_ref, main1, main2):
    for k_ref, main in ((k1_ref, main1), (k2_ref, main2)):
        for i in range(4):
            down, right = (i // 2) * 5 * FEAT, (i % 2) * FEAT
            main[down : down + 5 * FEAT, right : right + FEAT] = k_ref[i]


def info_kernel(pixel_ref, ray_ref, k1_ref, k2_ref, info_ref, main1, main2):
    arrange_taps(k1_ref, k2_ref, main1, main2)
    _, _, bundle = coordinates()
    pixel = pixel_ref[...]
    local_row = ((pixel >> 9) & (TH - 1)).astype(f32)
    local_col = (pixel & (TW - 1)).astype(f32)
    ray = ray_ref[...]
    lane_iota = iota((LANES, LANES), 0)
    iota8 = iota((8, LANES), 0)
    own = jnp.zeros((16, LANES), f32)
    for j in range(RAYS // LANES):
        at = ray[j : j + 1, :]
        mine = iota8 == (at >> 7)
        values = jnp.concatenate(
            [
                jnp.where(mine, local_row[j : j + 1, :], 0.0),
                jnp.where(mine, local_col[j : j + 1, :], 0.0),
            ],
            axis=0,
        ).astype(bf16)
        own = own + dot_nt(values, as_bf16(lane_iota == (at & (LANES - 1))))
    quarter = bundle & 3
    keep = (iota((16, LANES), 1) >> 5) == quarter
    for q in range(4):
        shift = ((quarter - q) & 3) * 32
        info_ref[q] = jnp.where(keep, pltpu.roll(own, shift, 1), 0.0)


def segment_kernel(
    live_smem,
    enc_ref,
    gap_ref,
    pixel_ref,
    ids_ref,
    w1_ref,
    b1_ref,
    w2_ref,
    b2_ref,
    wd_ref,
    wf_ref,
    near_hbm,
    far_hbm,
    ray_ref,
    spread,
    hidden,
    first_a,
    first_b,
    wide1,
    wide2,
    pre,
    depth,
    colour_a,
    colour_b,
    table_ref,
    pos_ref,
    pos_smem,
    staged,
    pos_sem,
    out_sems,
):
    step = pl.program_id(0)
    to_smem = pltpu.make_async_copy(pos_ref, pos_smem, pos_sem)
    half = SUPER * SAMPLES // 2

    @pl.when(step == 0)
    def _():
        zero = jnp.zeros((FEAT, FEAT), bf16)
        for wide, w in ((wide1, w1_ref), (wide2, w2_ref)):
            wide[:FEAT, :FEAT] = w[0]
            wide[:FEAT, FEAT:] = zero
            wide[FEAT:, :FEAT] = zero
            wide[FEAT:, FEAT:] = w[0]
        index_rays(pixel_ref, ids_ref, pos_ref, ray_ref)
        to_smem.start()

    bias1 = jnp.concatenate([b1_ref[...]] * 2, axis=1)
    bias2 = jnp.concatenate([b2_ref[...]] * 2, axis=1)
    head = wd_ref[...].astype(f32)
    lane8 = iota((SAMPLES, LANES), 1)
    chunk = RAYS // (SLOTS // SUPER * 4) * 8 + 8
    start = pl.multiple_of(jnp.minimum(step * chunk, RAYS - chunk), 8)
    spread[pl.ds(start, chunk), :] = jnp.zeros((chunk, FEAT), f32)

    def layer_one(base, out):
        x = jnp.concatenate(
            [enc_ref[base : base + half, :], enc_ref[base + half : base + 2 * half, :]], axis=1
        )
        out[...] = jnp.maximum((dot_nn(x, wide1[...]) + bias1).astype(bf16), 0.0)

    def layer_two(source, block):
        h2 = jnp.maximum(dot_nn(source[...], wide2[...]) + bias2, 0.0)
        hidden[pl.ds(pl.multiple_of(block * half, half), half), :] = h2.astype(bf16)
        for side in range(2):
            part = h2[:, side * FEAT : (side + 1) * FEAT] * head
            total = jnp.sum(part, axis=1, keepdims=True)
            lined = jnp.zeros((SAMPLES, LANES), f32)
            for s in range(LANES):
                lined = jnp.where(lane8 == s, total[SAMPLES * s : SAMPLES * (s + 1), :], lined)
            pre[2 * block + side] = lined

    layer_two(first_b, jnp.maximum(2 * step - 1, 0))
    layer_one(0, first_a)
    layer_two(first_a, 2 * step)
    layer_one(SUPER * SAMPLES, first_b)

    @pl.when(step == pl.num_programs(0) - 1)
    def _():
        live = live_smem[0]
        blocks = SLOTS // SUPER
        layer_two(first_b, blocks - 1)
        to_smem.wait()
        sample = iota((SAMPLES, LANES), 0)
        for b in range(SLOTS // LANES):
            v = pre[b]
            soft = jnp.maximum(v, 0.0) + jnp.log1p(jnp.exp(-jnp.abs(v)))
            opacity = soft * gap_ref[:, b * LANES : (b + 1) * LANES]
            inc = opacity
            for shift in (1, 2, 4):
                inc = inc + jnp.where(sample >= shift, pltpu.roll(inc, shift, 0), 0.0)
            weight = jnp.exp(opacity - inc) * (1.0 - jnp.exp(-opacity))
            alive = b * LANES + lane8 < live
            pre[b] = jnp.where(alive, weight, 0.0)
            depth[b : b + 1, :] = jnp.where(alive, inc, 0.0)[SAMPLES - 1 :, :]
        high_iota, low_iota = iota((RAYS // LANES, LANES), 0), iota((LANES, LANES), 0)

        def depth_table(block, table):
            for h in range(2):
                at = pos_ref[pl.ds(2 * block + h, 1), :]
                here = depth[pl.ds(2 * block + h, 1), :]
                coarse = here.astype(bf16).astype(f32)
                high = high_iota == (at >> 7)
                wanted = jnp.concatenate(
                    [jnp.where(high, coarse, 0.0), jnp.where(high, here - coarse, 0.0)], axis=0
                ).astype(bf16)
                table = table + dot_nt(wanted, as_bf16(low_iota == (at & (LANES - 1))))
            return table

        of_slot = iota((32, SUPER), 0) == (iota((32, SUPER), 1) >> 3)
        of_sample = as_bf16(iota((SAMPLES, SUPER), 0) == (iota((SAMPLES, SUPER), 1) & 7))

        def mix(block, colour):
            spaced = [
                lax.dot_general(
                    pre[2 * block + side].astype(bf16),
                    of_sample,
                    (((0,), (0,)), ((), ())),
                    preferred_element_type=f32,
                )
                for side in range(2)
            ]
            gathered = [None] * 8
            for i in range(4):
                rows = slice(32 * i, 32 * i + 32)
                both = jnp.concatenate(
                    [jnp.where(of_slot, spaced[side][rows], 0.0) for side in range(2)], axis=0
                ).astype(bf16)
                at = block * half + i * SUPER
                summed = dot_nn(both, hidden[pl.ds(at, SUPER), :])
                gathered[i] = summed[:32, :FEAT]
                gathered[i + 4] = summed[32:, FEAT:]
            mixed = jnp.concatenate(gathered, axis=0).astype(bf16)
            colour[...] = dot_nn(mixed, wf_ref[0])

        def scatter(block, colour):
            for s in range(SUPER):
                slot = block * SUPER + s
                at = pos_smem[slot // LANES, slot % LANES]
                spread[pl.ds(at, 1), :] = colour[s : s + 1, :]

        mix(0, colour_a)

        table_ref[...] = jnp.zeros_like(table_ref)
        for t in range(blocks // 2):

            @pl.when(live >= 0)
            def _(t=t):
                table = table_ref[...]
                mix(2 * t + 1, colour_b)
                scatter(2 * t, colour_a)
                table = depth_table(2 * t, table)
                if 2 * t + 2 < blocks:
                    mix(2 * t + 2, colour_a)
                scatter(2 * t + 1, colour_b)
                table_ref[...] = depth_table(2 * t + 1, table)

        table = table_ref[...]
        stores = []
        for n in range(8):
            k, g = 1 - n // 4, n % 4
            at = (4 * k + g) * PIECE
            staged[n, :PIECE, :] = spread[at : at + PIECE, :].astype(bf16)
            rows = (4 * k + g) * 8
            staged[n, PIECE:, :] = jnp.concatenate(
                [table[rows : rows + 8], table[64 + rows : 72 + rows]], axis=0
            ).astype(bf16)
            out = (near_hbm, far_hbm)[k].at[g]
            stores.append(pltpu.make_async_copy(staged.at[n], out, out_sems.at[n]))
            stores[-1].start()
        for store in stores:
            store.wait()


def read_depth(ref):
    rows = ref[PIECE:, :].astype(f32)
    return rows[:8] + rows[8:]


def scaled(ref, factors, i):
    return ref[i * LANES : (i + 1) * LANES, :].astype(f32) * factors[:, i : i + 1]


def pair_kernel(mine_hbm, arrived_hbm, o0, o1, o2, o3, mine, arrived, done, in_sems, out_sems):
    my_core, _, _ = coordinates()
    loads = [
        (
            pltpu.make_async_copy(mine_hbm.at[g], mine.at[g], in_sems.at[2 * g]),
            pltpu.make_async_copy(arrived_hbm.at[g], arrived.at[g], in_sems.at[2 * g + 1]),
        )
        for g in PAIR_ORDER
    ]
    for two in loads:
        for load in two:
            load.start()

    def combine(front_all, back_all):
        stores = []
        for g, two in zip(PAIR_ORDER, loads):
            for load in two:
                load.wait()
            front, back, out = front_all.at[g], back_all.at[g], done.at[g]
            d_front, d_back = read_depth(front), read_depth(back)
            fade = jnp.exp(-d_front).T
            for i in range(8):
                at = slice(i * LANES, (i + 1) * LANES)
                out[at, :] = (front[at, :].astype(f32) + scaled(back, fade, i)).astype(bf16)
            both = d_front + d_back
            coarse = both.astype(bf16).astype(f32)
            out[PIECE:, :] = jnp.concatenate([coarse, both - coarse], axis=0).astype(bf16)
            store = pltpu.make_async_copy(out, (o0, o1, o2, o3)[g], out_sems.at[g])
            store.start()
            stores.append(store)
        for store in stores:
            store.wait()

    @pl.when(my_core == 0)
    def _():
        combine(mine, arrived)

    @pl.when(my_core == 1)
    def _():
        combine(arrived, mine)


def merge_kernel(p0_ref, p1_ref, p2_ref, p3_ref, info_ref, out_ref):
    _, y, _ = coordinates()
    pieces = (p0_ref, p1_ref, p2_ref, p3_ref)
    places = [(y - k) & 3 for k in range(4)]
    depths = [read_depth(ref) for ref in pieces]
    factors = []
    for a in range(4):
        before = jnp.zeros_like(depths[0])
        for b in range(4):
            if b != a:
                before = before + jnp.where(places[b] < places[a], depths[b], 0.0)
        factors.append(jnp.exp(-before).T)
    for i in range(8):
        total = scaled(pieces[0], factors[0], i)
        for k in range(1, 4):
            total = total + scaled(pieces[k], factors[k], i)
        total = total.astype(bf16)
        for q in range(4):
            tile = i * 4 + q
            out_ref[tile, :32, :] = total[q * 32 : q * 32 + 32, :]
            extra = jnp.concatenate(
                [
                    info_ref[q, i : i + 1, :],
                    info_ref[q, i + 8 : i + 9, :],
                    jnp.zeros((6, LANES), f32),
                ],
                axis=0,
            )
            out_ref[tile, 32:, :] = extra.astype(bf16)


def place_kernel(in_ref, out_ref, left_ref, right_ref):
    total = jnp.zeros((TH * TW, FEAT), f32)
    pixel_iota = iota((TH * TW, LANES), 0)
    for g in range(8):
        rows = jnp.concatenate([in_ref[4 * g + q, :32, :] for q in range(4)], axis=0)
        place = in_ref[4 * g, 32:, :].astype(f32)
        for q in range(1, 4):
            place = place + in_ref[4 * g + q, 32:, :].astype(f32)
        pixel = (place[0:1, :] * TW + place[1:2, :]).astype(i32)
        total = total + dot_nn(as_bf16(pixel_iota == pixel), rows)
    out_ref[...] = total.astype(bf16)
    left_ref[...] = jnp.concatenate([total[y * TW : y * TW + 8] for y in range(TH)]).astype(bf16)
    right_ref[...] = jnp.concatenate(
        [total[y * TW + TW - 8 : y * TW + TW] for y in range(TH)]
    ).astype(bf16)


def whole(shape):
    return pl.BlockSpec(shape, lambda *_: (0,) * len(shape))


def shape_of(shape, dtype):
    return jax.ShapeDtypeStruct(shape, dtype)


VMEM = pl.BlockSpec(memory_space=pltpu.VMEM)
HBM = pl.BlockSpec(memory_space=pltpu.HBM)


def segments(live, enc, gaps, pixel, ids, w1, b1, w2, b2, wd, wf):
    rows = 2 * SUPER * SAMPLES
    out = shape_of((4, PACK, FEAT), bf16)
    return pl.pallas_call(
        segment_kernel,
        grid_spec=pltpu.PrefetchScalarGridSpec(
            num_scalar_prefetch=1,
            grid=(SLOTS * SAMPLES // rows,),
            in_specs=[pl.BlockSpec((rows, FEAT), lambda i, *_: (i, 0))]
            + [whole(a.shape) for a in (gaps, pixel, ids, w1, b1, w2, b2, wd, wf)],
            out_specs=[HBM, HBM, whole(pixel.shape)],
            scratch_shapes=[
                pltpu.VMEM((RAYS, FEAT), f32),
                pltpu.VMEM((SLOTS * SAMPLES // 2, 2 * FEAT), bf16),
                pltpu.VMEM((SUPER * SAMPLES // 2, 2 * FEAT), bf16),
                pltpu.VMEM((SUPER * SAMPLES // 2, 2 * FEAT), bf16),
                pltpu.VMEM((2 * FEAT, 2 * FEAT), bf16),
                pltpu.VMEM((2 * FEAT, 2 * FEAT), bf16),
                pltpu.VMEM((SLOTS // LANES, SAMPLES, LANES), f32),
                pltpu.VMEM((SLOTS // LANES, LANES), f32),
                pltpu.VMEM((SUPER, FEAT), f32),
                pltpu.VMEM((SUPER, FEAT), f32),
                pltpu.VMEM((2 * RAYS // LANES, LANES), f32),
                pltpu.VMEM((SLOTS // LANES, LANES), i32),
                pltpu.SMEM((SLOTS // LANES, LANES), i32),
                pltpu.VMEM((8, PACK, FEAT), bf16),
                pltpu.SemaphoreType.DMA,
                pltpu.SemaphoreType.DMA((8,)),
            ],
        ),
        out_shape=[out, out, shape_of(pixel.shape, i32)],
        name="segments",
    )(live, enc, gaps, pixel, ids, w1, b1, w2, b2, wd, wf)


def exchanged(low, high, axis):
    size = lax.axis_size(axis)
    up = [(i, i + 1) for i in range(size - 1)]
    down = [(j, i) for i, j in up]
    return lax.ppermute(high, axis, up), lax.ppermute(low, axis, down)


def image_rows(block_ref, left_ref, right_ref, y):
    return [
        left_ref[8 * y : 8 * y + 8, :].astype(f32),
        block_ref[TW * y : TW * y + TW, :].astype(f32),
        right_ref[8 * y : 8 * y + 8, :].astype(f32),
    ]


def fill(rows, at, block_ref, left_ref, right_ref, first, last):
    for y in range(first, last):
        left, mid, right = image_rows(block_ref, left_ref, right_ref, y)
        base = at + (y - first) * PITCH
        rows[base : base + 8, :] = left
        rows[base + 8 : base + 8 + TW, :] = mid
        rows[base + 8 + TW : base + PITCH, :] = right


def conv_rows(source, at, first, count, main_ref, last, bias, shifted, partial, emit):
    total = (count + 4) * PITCH
    for j in range(5):
        shifted[:total, j * FEAT : (j + 1) * FEAT] = source[
            at + first + j : at + first + j + total, :
        ].astype(bf16)
    span = (count + 1) * PITCH
    parts = 1 if count == 4 else 5
    size = span // parts
    for p in range(parts):
        rows = slice(p * size, (p + 1) * size)
        below = slice(p * size + 2 * PITCH, (p + 1) * size + 2 * PITCH)
        partial[rows, :] = dot_nn(shifted[rows, :], main_ref[: 5 * FEAT, :]) + dot_nn(
            shifted[below, :], main_ref[5 * FEAT :, :]
        )
    for p in range(count // 4):
        base = p * 4 * PITCH
        rows = slice(base, base + 4 * PITCH)
        low = slice(base + PITCH, base + 5 * PITCH)
        end = slice(base + 4 * PITCH, base + 8 * PITCH)
        emit(
            p,
            partial[rows, :FEAT]
            + partial[low, FEAT:]
            + (dot_nn(shifted[end, :], last) + bias),
        )


def hidden_rows(value, first_row):
    flat = iota((4 * PITCH, FEAT), 0)
    col = lax.axis_index("depth") * TW - 2 + flat % PITCH
    row = lax.axis_index("rays") * TH + first_row + flat // PITCH
    inside = (row >= 0) & (row < HEIGHT) & (col >= 0) & (col < WIDE)
    return jnp.where(inside, jnp.maximum(value, 0.0), 0.0)


def inner_kernel(
    block_ref, left_ref, right_ref, main_ref, k_ref, b_ref, out_ref, rows, shifted, partial
):
    fill(rows, 0, block_ref, left_ref, right_ref, 0, TH)
    rows[TH * PITCH :, :] = jnp.zeros((16, FEAT), f32)

    def emit(p, value):
        out_ref[p * 4 * PITCH : (p + 1) * 4 * PITCH, :] = hidden_rows(value, 2 + 4 * p).astype(bf16)

    conv_rows(rows, 0, 4, 12, main_ref, k_ref[4], b_ref[...], shifted, partial, emit)


def outer_kernel(
    block_ref,
    left_ref,
    right_ref,
    above_ref,
    below_ref,
    inner_ref,
    main1_ref,
    k1_ref,
    b1_ref,
    main2_ref,
    k2_ref,
    b2_ref,
    out_ref,
    rows,
    hidden,
    shifted,
    partial,
):
    quad = 4 * PITCH
    rows[:quad, :] = above_ref[...].astype(f32)
    fill(rows, quad, block_ref, left_ref, right_ref, 0, 4)
    rows[2 * quad : 2 * quad + 16, :] = jnp.zeros((16, FEAT), f32)
    second = 2 * quad + 16
    fill(rows, second, block_ref, left_ref, right_ref, TH - 4, TH)
    rows[second + quad : second + 2 * quad, :] = below_ref[...].astype(f32)
    rows[second + 2 * quad :, :] = jnp.zeros((16, FEAT), f32)
    hidden[quad : 4 * quad, :] = inner_ref[...].astype(f32)
    hidden[5 * quad :, :] = jnp.zeros((16, FEAT), f32)
    for n, (at, first_row) in enumerate(((0, -2), (second, TH - 2))):

        def emit(p, value, n=n, first_row=first_row):
            hidden[4 * n * quad : (4 * n + 1) * quad, :] = hidden_rows(value, first_row)

        conv_rows(
            rows, at, 4, 4, main1_ref, k1_ref[4], b1_ref[...], shifted.at[n], partial.at[n], emit
        )

    def finish(p, value):
        value = value.astype(bf16)
        for y in range(4):
            out_ref[p * 4 + y] = value[y * PITCH : y * PITCH + TW, :]

    conv_rows(
        hidden, 0, 0, TH, main2_ref, k2_ref[4], b2_ref[...], shifted.at[2], partial.at[2], finish
    )


def on_device(
    encodings,
    spacing,
    ray_ids,
    live_count,
    pixel_of_ray,
    w_first,
    b_first,
    w_second,
    b_second,
    w_density,
    w_feature,
    kernel_one,
    bias_one,
    kernel_two,
    bias_two,
):
    pixel = pixel_of_ray.reshape(RAYS // LANES, LANES)
    near, far, ray = segments(
        live_count.reshape(1),
        encodings.reshape(SLOTS * SAMPLES, FEAT),
        spacing[0],
        pixel,
        ray_ids.reshape(SLOTS // LANES, LANES),
        w_first,
        b_first,
        w_second,
        b_second,
        w_density,
        w_feature,
    )
    arrived = lax.ppermute(far, "depth", [(i, i ^ 1) for i in range(8)])
    piece = shape_of((PACK, FEAT), bf16)
    pieces = pl.pallas_call(
        pair_kernel,
        in_specs=[HBM] * 2,
        out_specs=[HBM] * 4,
        out_shape=[piece] * 4,
        scratch_shapes=[pltpu.VMEM((4, PACK, FEAT), bf16)] * 3
        + [pltpu.SemaphoreType.DMA((8,)), pltpu.SemaphoreType.DMA((4,))],
        name="pair",
    )(near, arrived)
    got = [
        lax.ppermute(pieces[k], "depth", [(i, (i + 2 * k) % 8) for i in range(8)])
        for k in range(1, 4)
    ]
    taps1, taps2 = kernel_one.reshape(5, 5 * FEAT, FEAT), kernel_two.reshape(5, 5 * FEAT, FEAT)
    main = shape_of((10 * FEAT, 2 * FEAT), bf16)
    info, main1, main2 = pl.pallas_call(
        info_kernel,
        in_specs=[VMEM] * 4,
        out_specs=[VMEM] * 3,
        out_shape=[shape_of((4, 16, LANES), f32), main, main],
        name="info",
    )(pixel, ray, taps1, taps2)
    outgoing = pl.pallas_call(
        merge_kernel,
        in_specs=[VMEM] * 5,
        out_specs=VMEM,
        out_shape=shape_of((32, 40, FEAT), bf16),
        name="merge",
    )(pieces[0], *got, info)
    incoming = lax.all_to_all(outgoing, "rays", split_axis=0, concat_axis=0, tiled=True)
    edge = shape_of((TH * 8, FEAT), bf16)
    block, low_edge, high_edge = pl.pallas_call(
        place_kernel,
        in_specs=[VMEM],
        out_specs=[VMEM] * 3,
        out_shape=[shape_of((TH * TW, FEAT), bf16), edge, edge],
        name="place",
    )(incoming)
    left, right = exchanged(low_edge, high_edge, "depth")
    parts = [left.reshape(TH, 8, FEAT), block.reshape(TH, TW, FEAT), right.reshape(TH, 8, FEAT)]
    first = jnp.concatenate([p[:HALO] for p in parts], axis=1).reshape(HALO * PITCH, FEAT)
    last = jnp.concatenate([p[TH - HALO :] for p in parts], axis=1).reshape(HALO * PITCH, FEAT)
    above, below = exchanged(first, last, "rays")
    inner = pl.pallas_call(
        inner_kernel,
        in_specs=[VMEM] * 6,
        out_specs=VMEM,
        out_shape=shape_of((12 * PITCH, FEAT), bf16),
        scratch_shapes=[
            pltpu.VMEM((TH * PITCH + 16, FEAT), f32),
            pltpu.VMEM((TH * PITCH, 5 * FEAT), bf16),
            pltpu.VMEM((13 * PITCH, 2 * FEAT), f32),
        ],
        name="inner",
    )(block, left, right, main1, taps1, bias_one[None])
    return pl.pallas_call(
        outer_kernel,
        in_specs=[VMEM] * 12,
        out_specs=VMEM,
        out_shape=shape_of((TH, TW, FEAT), bf16),
        scratch_shapes=[
            pltpu.VMEM((16 * PITCH + 32, FEAT), f32),
            pltpu.VMEM((20 * PITCH + 16, FEAT), f32),
            pltpu.VMEM((3, 20 * PITCH, 5 * FEAT), bf16),
            pltpu.VMEM((3, 17 * PITCH, 2 * FEAT), f32),
        ],
        name="outer",
    )(
        block,
        left,
        right,
        above,
        below,
        inner,
        main1,
        taps1,
        bias_one[None],
        main2,
        taps2,
        bias_two[None],
    )


def solution(mesh):
    in_specs = (
        P("depth", "rays", None, None),
        P("depth", None, "rays"),
        P("depth", "rays"),
        P("depth", "rays"),
        P("rays"),
        P("depth", None, None),
        P("depth", None),
        P("depth", None, None),
        P("depth", None),
        P("depth", None),
        P("depth", None, None),
        P(),
        P(),
        P(),
        P(),
    )
    return jax.shard_map(
        on_device, mesh=mesh, in_specs=in_specs, out_specs=P("rays", "depth", None), check_vma=False
    )
```

```python
import functools

import jax
import jax.numpy as jnp
from jax import lax
from jax.experimental import pallas as pl
from jax.experimental.pallas import tpu as pltpu
from jax.sharding import PartitionSpec as P

FEAT = 128
SAMPLES = 8
TH = 16
TW = 64
WIDE = 512
HEIGHT = 512
SLOTS = 5120
RAYS = 8192
LANES = 128
HALO = 4
PITCH = TW + 16
SMALL = pltpu.CompilerParams(vmem_limit_bytes=24 << 20)
PIECE = 1024
PACK = PIECE + 16
SUPER = 256
f32 = jnp.float32
bf16 = jnp.bfloat16
i32 = jnp.int32


def dot_nt(lhs, rhs):
    return lax.dot_general(lhs, rhs, (((1,), (1,)), ((), ())), preferred_element_type=f32)


def dot_nn(lhs, rhs):
    return jnp.dot(lhs, rhs, preferred_element_type=f32)


def iota(shape, axis):
    return lax.broadcasted_iota(i32, shape, axis)


def as_bf16(mask):
    return jnp.where(mask, 1.0, 0.0).astype(bf16)


def coordinates():
    place = lax.axis_index("depth")
    return place & 1, place >> 1, lax.axis_index("rays")


def rank_sum(parts):
    total = parts[0]
    for part in parts[1:]:
        total = total + part
    return jnp.sum(total, axis=0, keepdims=True)


def index_rays(pixel_ref, ids_ref, pos_ref, ray_ref):
    my_core, my_y, _ = coordinates()
    pixel = pixel_ref[...]
    row, col = pixel >> 9, pixel & (WIDE - 1)
    block_col = col >> 6
    core_rel = (block_col & 1) ^ my_core
    y_rel = ((block_col >> 1) - my_y) & 3
    group = core_rel * 128 + y_rel * 32 + (row >> 4)
    column = group.astype(f32).T.astype(i32)
    earlier = iota((LANES, LANES), 0) < iota((LANES, LANES), 1)
    iota16 = iota((16, LANES), 0)
    seen = jnp.zeros((16, 16), f32)
    ranks = []
    for j in range(RAYS // LANES):
        g = group[j : j + 1, :]
        same = jnp.where((column[:, j : j + 1] == g) & earlier, 1.0, 0.0)
        coarse = as_bf16(iota16 == (g >> 4))
        fine = iota16 == (g & 15)
        found = jnp.where(fine, dot_nn(seen.astype(bf16), coarse), 0.0)
        seen = seen + dot_nt(as_bf16(fine), coarse)
        parts = [same[8 * k : 8 * k + 8] for k in range(16)] + [found[:8], found[8:]]
        ranks.append(rank_sum(parts))
    rank = jnp.concatenate(ranks, axis=0).astype(i32)
    high = group >> 2
    low = (group & 3) * 32 + rank
    ray_ref[...] = high * LANES + low
    table = jnp.concatenate(
        [(high * LANES).astype(f32).T, low.astype(f32).T], axis=1
    ).astype(bf16)
    high_iota = iota((RAYS // LANES, LANES), 0)
    lane_iota = iota((LANES, LANES), 0)
    for j in range(SLOTS // LANES):
        ids = ids_ref[j : j + 1, :]
        hot = as_bf16(high_iota == (ids >> 7))
        found = dot_nn(table, jnp.concatenate([hot, hot], axis=0))
        found = jnp.where(lane_iota == (ids & (LANES - 1)), found, 0.0)
        pos_ref[j : j + 1, :] = rank_sum([found[8 * k : 8 * k + 8] for k in range(16)]).astype(i32)


def arrange_taps(k1_ref, k2_ref, main1, main2):
    for k_ref, main in ((k1_ref, main1), (k2_ref, main2)):
        for i in range(4):
            down, right = (i // 2) * 5 * FEAT, (i % 2) * FEAT
            main[down : down + 5 * FEAT, right : right + FEAT] = k_ref[i]


def info_kernel(pixel_ref, ray_ref, k1_ref, k2_ref, info_ref, main1, main2):
    arrange_taps(k1_ref, k2_ref, main1, main2)
    _, _, bundle = coordinates()
    pixel = pixel_ref[...]
    local_row = ((pixel >> 9) & (TH - 1)).astype(f32)
    local_col = (pixel & (TW - 1)).astype(f32)
    ray = ray_ref[...]
    lane_iota = iota((LANES, LANES), 0)
    iota8 = iota((8, LANES), 0)
    own = jnp.zeros((16, LANES), f32)
    for j in range(RAYS // LANES):
        at = ray[j : j + 1, :]
        mine = iota8 == (at >> 7)
        values = jnp.concatenate(
            [
                jnp.where(mine, local_row[j : j + 1, :], 0.0),
                jnp.where(mine, local_col[j : j + 1, :], 0.0),
            ],
            axis=0,
        ).astype(bf16)
        own = own + dot_nt(values, as_bf16(lane_iota == (at & (LANES - 1))))
    quarter = bundle & 3
    keep = (iota((16, LANES), 1) >> 5) == quarter
    for q in range(4):
        shift = ((quarter - q) & 3) * 32
        info_ref[q] = jnp.where(keep, pltpu.roll(own, shift, 1), 0.0)


def segment_kernel(
    live_smem,
    enc_ref,
    gap_ref,
    pixel_ref,
    ids_ref,
    w1_ref,
    b1_ref,
    w2_ref,
    b2_ref,
    wd_ref,
    wf_ref,
    near_ref,
    far_ref,
    ray_ref,
    spread,
    hidden,
    first_a,
    first_b,
    wide1,
    wide2,
    pre,
    depth,
    colour_a,
    colour_b,
    table_ref,
    pos_ref,
    pos_smem,
    pos_sem,
):
    step = pl.program_id(0)
    to_smem = pltpu.make_async_copy(pos_ref, pos_smem, pos_sem)
    half = SUPER * SAMPLES // 2

    @pl.when(step == 0)
    def _():
        zero = jnp.zeros((FEAT, FEAT), bf16)
        for wide, w in ((wide1, w1_ref), (wide2, w2_ref)):
            wide[:FEAT, :FEAT] = w[0]
            wide[:FEAT, FEAT:] = zero
            wide[FEAT:, :FEAT] = zero
            wide[FEAT:, FEAT:] = w[0]
        index_rays(pixel_ref, ids_ref, pos_ref, ray_ref)
        to_smem.start()

    bias1 = jnp.concatenate([b1_ref[...]] * 2, axis=1)
    bias2 = jnp.concatenate([b2_ref[...]] * 2, axis=1)
    head = wd_ref[...].astype(f32)
    lane8 = iota((SAMPLES, LANES), 1)
    chunk = RAYS // (SLOTS // SUPER * 4) * 8 + 8
    start = pl.multiple_of(jnp.minimum(step * chunk, RAYS - chunk), 8)
    spread[pl.ds(start, chunk), :] = jnp.zeros((chunk, FEAT), f32)

    def layer_one(base, out):
        x = jnp.concatenate(
            [enc_ref[base : base + half, :], enc_ref[base + half : base + 2 * half, :]], axis=1
        )
        out[...] = jnp.maximum((dot_nn(x, wide1[...]) + bias1).astype(bf16), 0.0)

    def layer_two(source, block):
        h2 = jnp.maximum(dot_nn(source[...], wide2[...]) + bias2, 0.0)
        hidden[pl.ds(pl.multiple_of(block * half, half), half), :] = h2.astype(bf16)
        for side in range(2):
            part = h2[:, side * FEAT : (side + 1) * FEAT] * head
            total = jnp.sum(part, axis=1, keepdims=True)
            lined = jnp.zeros((SAMPLES, LANES), f32)
            for s in range(LANES):
                lined = jnp.where(lane8 == s, total[SAMPLES * s : SAMPLES * (s + 1), :], lined)
            pre[2 * block + side] = lined

    layer_two(first_b, jnp.maximum(2 * step - 1, 0))
    layer_one(0, first_a)
    layer_two(first_a, 2 * step)
    layer_one(SUPER * SAMPLES, first_b)

    @pl.when(step == pl.num_programs(0) - 1)
    def _():
        live = live_smem[0]
        blocks = SLOTS // SUPER
        layer_two(first_b, blocks - 1)
        to_smem.wait()
        sample = iota((SAMPLES, LANES), 0)
        for b in range(SLOTS // LANES):
            v = pre[b]
            soft = jnp.maximum(v, 0.0) + jnp.log1p(jnp.exp(-jnp.abs(v)))
            opacity = soft * gap_ref[:, b * LANES : (b + 1) * LANES]
            inc = opacity
            for shift in (1, 2, 4):
                inc = inc + jnp.where(sample >= shift, pltpu.roll(inc, shift, 0), 0.0)
            weight = jnp.exp(opacity - inc) * (1.0 - jnp.exp(-opacity))
            alive = b * LANES + lane8 < live
            pre[b] = jnp.where(alive, weight, 0.0)
            depth[b : b + 1, :] = jnp.where(alive, inc, 0.0)[SAMPLES - 1 :, :]
        high_iota, low_iota = iota((RAYS // LANES, LANES), 0), iota((LANES, LANES), 0)

        def depth_table(block, table):
            for h in range(2):
                at = pos_ref[pl.ds(2 * block + h, 1), :]
                here = depth[pl.ds(2 * block + h, 1), :]
                coarse = here.astype(bf16).astype(f32)
                high = high_iota == (at >> 7)
                wanted = jnp.concatenate(
                    [jnp.where(high, coarse, 0.0), jnp.where(high, here - coarse, 0.0)], axis=0
                ).astype(bf16)
                table = table + dot_nt(wanted, as_bf16(low_iota == (at & (LANES - 1))))
            return table

        of_slot = iota((32, SUPER), 0) == (iota((32, SUPER), 1) >> 3)
        of_sample = as_bf16(iota((SAMPLES, SUPER), 0) == (iota((SAMPLES, SUPER), 1) & 7))

        def mix(block, colour):
            spaced = [
                lax.dot_general(
                    pre[2 * block + side].astype(bf16),
                    of_sample,
                    (((0,), (0,)), ((), ())),
                    preferred_element_type=f32,
                )
                for side in range(2)
            ]
            gathered = [None] * 8
            for i in range(4):
                rows = slice(32 * i, 32 * i + 32)
                both = jnp.concatenate(
                    [jnp.where(of_slot, spaced[side][rows], 0.0) for side in range(2)], axis=0
                ).astype(bf16)
                at = block * half + i * SUPER
                summed = dot_nn(both, hidden[pl.ds(at, SUPER), :])
                gathered[i] = summed[:32, :FEAT]
                gathered[i + 4] = summed[32:, FEAT:]
            mixed = jnp.concatenate(gathered, axis=0).astype(bf16)
            colour[...] = dot_nn(mixed, wf_ref[0])

        def scatter(block, colour):
            for s in range(SUPER):
                slot = block * SUPER + s
                at = pos_smem[slot // LANES, slot % LANES]
                spread[pl.ds(at, 1), :] = colour[s : s + 1, :]

        mix(0, colour_a)

        table_ref[...] = jnp.zeros_like(table_ref)
        for t in range(blocks // 2):

            @pl.when(live >= 0)
            def _(t=t):
                table = table_ref[...]
                mix(2 * t + 1, colour_b)
                scatter(2 * t, colour_a)
                table = depth_table(2 * t, table)
                if 2 * t + 2 < blocks:
                    mix(2 * t + 2, colour_a)
                scatter(2 * t + 1, colour_b)
                table_ref[...] = depth_table(2 * t + 1, table)

        table = table_ref[...]
        for n in range(8):
            k, g = 1 - n // 4, n % 4
            at = (4 * k + g) * PIECE
            out = (near_ref, far_ref)[k]
            out[g, :PIECE, :] = spread[at : at + PIECE, :].astype(bf16)
            rows = (4 * k + g) * 8
            out[g, PIECE:, :] = jnp.concatenate(
                [table[rows : rows + 8], table[64 + rows : 72 + rows]], axis=0
            ).astype(bf16)


def read_depth(ref):
    rows = ref[PIECE:, :].astype(f32)
    return rows[:8] + rows[8:]


def scaled(ref, factors, i):
    return ref[i * LANES : (i + 1) * LANES, :].astype(f32) * factors[:, i : i + 1]


def pair_kernel(mine, arrived, o0, o1, o2, o3):
    my_core, _, _ = coordinates()
    def combine(front_all, back_all):
        for g in range(4):
            front, back, out = front_all.at[g], back_all.at[g], (o0, o1, o2, o3)[g]
            d_front, d_back = read_depth(front), read_depth(back)
            fade = jnp.exp(-d_front).T
            for i in range(8):
                at = slice(i * LANES, (i + 1) * LANES)
                out[at, :] = (front[at, :].astype(f32) + scaled(back, fade, i)).astype(bf16)
            both = d_front + d_back
            coarse = both.astype(bf16).astype(f32)
            out[PIECE:, :] = jnp.concatenate([coarse, both - coarse], axis=0).astype(bf16)

    @pl.when(my_core == 0)
    def _():
        combine(mine, arrived)

    @pl.when(my_core == 1)
    def _():
        combine(arrived, mine)


def merge_kernel(p0_ref, p1_ref, p2_ref, p3_ref, info_ref, out_ref):
    _, y, _ = coordinates()
    pieces = (p0_ref, p1_ref, p2_ref, p3_ref)
    places = [(y - k) & 3 for k in range(4)]
    depths = [read_depth(ref) for ref in pieces]
    factors = []
    for a in range(4):
        before = jnp.zeros_like(depths[0])
        for b in range(4):
            if b != a:
                before = before + jnp.where(places[b] < places[a], depths[b], 0.0)
        factors.append(jnp.exp(-before).T)
    for i in range(8):
        total = scaled(pieces[0], factors[0], i)
        for k in range(1, 4):
            total = total + scaled(pieces[k], factors[k], i)
        total = total.astype(bf16)
        for q in range(4):
            tile = i * 4 + q
            out_ref[tile, :32, :] = total[q * 32 : q * 32 + 32, :]
            extra = jnp.concatenate(
                [
                    info_ref[q, i : i + 1, :],
                    info_ref[q, i + 8 : i + 9, :],
                    jnp.zeros((6, LANES), f32),
                ],
                axis=0,
            )
            out_ref[tile, 32:, :] = extra.astype(bf16)


def place_kernel(in_ref, out_ref, left_ref, right_ref):
    total = jnp.zeros((TH * TW, FEAT), f32)
    pixel_iota = iota((TH * TW, LANES), 0)
    for g in range(8):
        rows = jnp.concatenate([in_ref[4 * g + q, :32, :] for q in range(4)], axis=0)
        place = in_ref[4 * g, 32:, :].astype(f32)
        for q in range(1, 4):
            place = place + in_ref[4 * g + q, 32:, :].astype(f32)
        pixel = (place[0:1, :] * TW + place[1:2, :]).astype(i32)
        total = total + dot_nn(as_bf16(pixel_iota == pixel), rows)
    out_ref[...] = total.astype(bf16)
    left_ref[...] = jnp.concatenate([total[y * TW : y * TW + 8] for y in range(TH)]).astype(bf16)
    right_ref[...] = jnp.concatenate(
        [total[y * TW + TW - 8 : y * TW + TW] for y in range(TH)]
    ).astype(bf16)


def on_chip(array):
    return pltpu.with_memory_space_constraint(array, pltpu.VMEM)


def off_chip(array):
    return pltpu.with_memory_space_constraint(array, pltpu.HBM)


def whole(shape):
    return pl.BlockSpec(shape, lambda *_: (0,) * len(shape))


def shape_of(shape, dtype):
    return jax.ShapeDtypeStruct(shape, dtype)


VMEM = pl.BlockSpec(memory_space=pltpu.VMEM)


def segments(live, enc, gaps, pixel, ids, w1, b1, w2, b2, wd, wf):
    rows = 2 * SUPER * SAMPLES
    out = pltpu.VMEM((4, PACK, FEAT), bf16)
    return pl.pallas_call(
        segment_kernel,
        grid_spec=pltpu.PrefetchScalarGridSpec(
            num_scalar_prefetch=1,
            grid=(SLOTS * SAMPLES // rows,),
            in_specs=[pl.BlockSpec((rows, FEAT), lambda i, *_: (i, 0))]
            + [whole(a.shape) for a in (gaps, pixel, ids, w1, b1, w2, b2, wd, wf)],
            out_specs=[VMEM, VMEM, whole(pixel.shape)],
            scratch_shapes=[
                pltpu.VMEM((RAYS, FEAT), f32),
                pltpu.VMEM((SLOTS * SAMPLES // 2, 2 * FEAT), bf16),
                pltpu.VMEM((SUPER * SAMPLES // 2, 2 * FEAT), bf16),
                pltpu.VMEM((SUPER * SAMPLES // 2, 2 * FEAT), bf16),
                pltpu.VMEM((2 * FEAT, 2 * FEAT), bf16),
                pltpu.VMEM((2 * FEAT, 2 * FEAT), bf16),
                pltpu.VMEM((SLOTS // LANES, SAMPLES, LANES), f32),
                pltpu.VMEM((SLOTS // LANES, LANES), f32),
                pltpu.VMEM((SUPER, FEAT), f32),
                pltpu.VMEM((SUPER, FEAT), f32),
                pltpu.VMEM((2 * RAYS // LANES, LANES), f32),
                pltpu.VMEM((SLOTS // LANES, LANES), i32),
                pltpu.SMEM((SLOTS // LANES, LANES), i32),
                pltpu.SemaphoreType.DMA,
            ],
        ),
        out_shape=[out, out, shape_of(pixel.shape, i32)],
        compiler_params=pltpu.CompilerParams(vmem_limit_bytes=40 << 20),
        name="segments",
    )(live, *[off_chip(a) for a in (enc, gaps, pixel, ids, w1, b1, w2, b2, wd, wf)])


def exchanged(low, high, axis):
    size = lax.axis_size(axis)
    up = [(i, i + 1) for i in range(size - 1)]
    down = [(j, i) for i, j in up]
    return lax.ppermute(high, axis, up), lax.ppermute(low, axis, down)


def image_rows(block_ref, left_ref, right_ref, y):
    return [
        left_ref[8 * y : 8 * y + 8, :].astype(f32),
        block_ref[TW * y : TW * y + TW, :].astype(f32),
        right_ref[8 * y : 8 * y + 8, :].astype(f32),
    ]


def fill(rows, at, block_ref, left_ref, right_ref, first, last):
    for y in range(first, last):
        left, mid, right = image_rows(block_ref, left_ref, right_ref, y)
        base = at + (y - first) * PITCH
        rows[base : base + 8, :] = left
        rows[base + 8 : base + 8 + TW, :] = mid
        rows[base + 8 + TW : base + PITCH, :] = right


def conv_rows(source, at, first, count, main_ref, last, bias, shifted, partial, emit):
    total = (count + 4) * PITCH
    for j in range(5):
        shifted[:total, j * FEAT : (j + 1) * FEAT] = source[
            at + first + j : at + first + j + total, :
        ].astype(bf16)
    span = (count + 1) * PITCH
    parts = 1 if count == 4 else 5
    size = span // parts
    for p in range(parts):
        rows = slice(p * size, (p + 1) * size)
        below = slice(p * size + 2 * PITCH, (p + 1) * size + 2 * PITCH)
        partial[rows, :] = dot_nn(shifted[rows, :], main_ref[: 5 * FEAT, :]) + dot_nn(
            shifted[below, :], main_ref[5 * FEAT :, :]
        )
    for p in range(count // 4):
        base = p * 4 * PITCH
        rows = slice(base, base + 4 * PITCH)
        low = slice(base + PITCH, base + 5 * PITCH)
        end = slice(base + 4 * PITCH, base + 8 * PITCH)
        emit(
            p,
            partial[rows, :FEAT]
            + partial[low, FEAT:]
            + (dot_nn(shifted[end, :], last) + bias),
        )


def hidden_rows(value, first_row):
    flat = iota((4 * PITCH, FEAT), 0)
    col = lax.axis_index("depth") * TW - 2 + flat % PITCH
    row = lax.axis_index("rays") * TH + first_row + flat // PITCH
    inside = (row >= 0) & (row < HEIGHT) & (col >= 0) & (col < WIDE)
    return jnp.where(inside, jnp.maximum(value, 0.0), 0.0)


def inner_kernel(
    block_ref, left_ref, right_ref, main_ref, k_ref, b_ref, out_ref, rows, shifted, partial
):
    fill(rows, 0, block_ref, left_ref, right_ref, 0, TH)
    rows[TH * PITCH :, :] = jnp.zeros((16, FEAT), f32)

    def emit(p, value):
        out_ref[p * 4 * PITCH : (p + 1) * 4 * PITCH, :] = hidden_rows(value, 2 + 4 * p).astype(bf16)

    conv_rows(rows, 0, 4, 12, main_ref, k_ref[4], b_ref[...], shifted, partial, emit)


def outer_kernel(
    block_ref,
    left_ref,
    right_ref,
    above_ref,
    below_ref,
    inner_ref,
    main1_ref,
    k1_ref,
    b1_ref,
    main2_ref,
    k2_ref,
    b2_ref,
    out_ref,
    rows,
    hidden,
    shifted,
    partial,
):
    quad = 4 * PITCH
    rows[:quad, :] = above_ref[...].astype(f32)
    fill(rows, quad, block_ref, left_ref, right_ref, 0, 4)
    rows[2 * quad : 2 * quad + 16, :] = jnp.zeros((16, FEAT), f32)
    second = 2 * quad + 16
    fill(rows, second, block_ref, left_ref, right_ref, TH - 4, TH)
    rows[second + quad : second + 2 * quad, :] = below_ref[...].astype(f32)
    rows[second + 2 * quad :, :] = jnp.zeros((16, FEAT), f32)
    hidden[quad : 4 * quad, :] = inner_ref[...].astype(f32)
    hidden[5 * quad :, :] = jnp.zeros((16, FEAT), f32)
    for n, (at, first_row) in enumerate(((0, -2), (second, TH - 2))):

        def emit(p, value, n=n, first_row=first_row):
            hidden[4 * n * quad : (4 * n + 1) * quad, :] = hidden_rows(value, first_row)

        conv_rows(
            rows, at, 4, 4, main1_ref, k1_ref[4], b1_ref[...], shifted.at[n], partial.at[n], emit
        )

    def finish(p, value):
        value = value.astype(bf16)
        for y in range(4):
            out_ref[p * 4 + y] = value[y * PITCH : y * PITCH + TW, :]

    conv_rows(
        hidden, 0, 0, TH, main2_ref, k2_ref[4], b2_ref[...], shifted.at[2], partial.at[2], finish
    )


def on_device(
    encodings,
    spacing,
    ray_ids,
    live_count,
    pixel_of_ray,
    w_first,
    b_first,
    w_second,
    b_second,
    w_density,
    w_feature,
    kernel_one,
    bias_one,
    kernel_two,
    bias_two,
):
    pixel = pixel_of_ray.reshape(RAYS // LANES, LANES)
    near, far, ray = segments(
        live_count.reshape(1),
        encodings.reshape(SLOTS * SAMPLES, FEAT),
        spacing[0],
        pixel,
        ray_ids.reshape(SLOTS // LANES, LANES),
        w_first,
        b_first,
        w_second,
        b_second,
        w_density,
        w_feature,
    )
    arrived = lax.ppermute(far, "depth", [(i, i ^ 1) for i in range(8)])
    piece = pltpu.VMEM((PACK, FEAT), bf16)
    pieces = pl.pallas_call(
        pair_kernel,
        in_specs=[VMEM] * 2,
        out_specs=[VMEM] * 4,
        out_shape=[piece] * 4,
        compiler_params=SMALL,
        name="pair",
    )(near, on_chip(arrived))
    got = [
        lax.ppermute(pieces[k], "depth", [(i, (i + 2 * k) % 8) for i in range(8)])
        for k in range(1, 4)
    ]
    taps1, taps2 = kernel_one.reshape(5, 5 * FEAT, FEAT), kernel_two.reshape(5, 5 * FEAT, FEAT)
    main = pltpu.VMEM((10 * FEAT, 2 * FEAT), bf16)
    info, main1, main2 = pl.pallas_call(
        info_kernel,
        in_specs=[VMEM] * 4,
        out_specs=[VMEM] * 3,
        out_shape=[pltpu.VMEM((4, 16, LANES), f32), main, main],
        compiler_params=SMALL,
        name="info",
    )(pixel, ray, taps1, taps2)
    outgoing = pl.pallas_call(
        merge_kernel,
        in_specs=[VMEM] * 5,
        out_specs=VMEM,
        out_shape=pltpu.VMEM((32, 40, FEAT), bf16),
        compiler_params=SMALL,
        name="merge",
    )(pieces[0], *[on_chip(g) for g in got], info)
    incoming = lax.all_to_all(outgoing, "rays", split_axis=0, concat_axis=0, tiled=True)
    edge = shape_of((TH * 8, FEAT), bf16)
    block, low_edge, high_edge = pl.pallas_call(
        place_kernel,
        in_specs=[VMEM],
        out_specs=[VMEM] * 3,
        out_shape=[shape_of((TH * TW, FEAT), bf16), edge, edge],
        compiler_params=SMALL,
        name="place",
    )(on_chip(incoming))
    left, right = exchanged(low_edge, high_edge, "depth")
    parts = [left.reshape(TH, 8, FEAT), block.reshape(TH, TW, FEAT), right.reshape(TH, 8, FEAT)]
    first = jnp.concatenate([p[:HALO] for p in parts], axis=1).reshape(HALO * PITCH, FEAT)
    last = jnp.concatenate([p[TH - HALO :] for p in parts], axis=1).reshape(HALO * PITCH, FEAT)
    above, below = exchanged(first, last, "rays")
    above, below = on_chip(above), on_chip(below)
    left, right = on_chip(left), on_chip(right)
    inner = pl.pallas_call(
        inner_kernel,
        in_specs=[VMEM] * 6,
        out_specs=VMEM,
        out_shape=pltpu.VMEM((12 * PITCH, FEAT), bf16),
        scratch_shapes=[
            pltpu.VMEM((TH * PITCH + 16, FEAT), f32),
            pltpu.VMEM((TH * PITCH, 5 * FEAT), bf16),
            pltpu.VMEM((13 * PITCH, 2 * FEAT), f32),
        ],
        compiler_params=SMALL,
        name="inner",
    )(block, left, right, main1, taps1, bias_one[None])
    return pl.pallas_call(
        outer_kernel,
        in_specs=[VMEM] * 12,
        out_specs=VMEM,
        out_shape=shape_of((TH, TW, FEAT), bf16),
        scratch_shapes=[
            pltpu.VMEM((16 * PITCH + 32, FEAT), f32),
            pltpu.VMEM((20 * PITCH + 16, FEAT), f32),
            pltpu.VMEM((3, 20 * PITCH, 5 * FEAT), bf16),
            pltpu.VMEM((3, 17 * PITCH, 2 * FEAT), f32),
        ],
        compiler_params=SMALL,
        name="outer",
    )(
        block,
        left,
        right,
        above,
        below,
        inner,
        main1,
        taps1,
        bias_one[None],
        main2,
        taps2,
        bias_two[None],
    )


def solution(mesh):
    in_specs = (
        P("depth", "rays", None, None),
        P("depth", None, "rays"),
        P("depth", "rays"),
        P("depth", "rays"),
        P("rays"),
        P("depth", None, None),
        P("depth", None),
        P("depth", None, None),
        P("depth", None),
        P("depth", None),
        P("depth", None, None),
        P(),
        P(),
        P(),
        P(),
    )
    return jax.shard_map(
        on_device, mesh=mesh, in_specs=in_specs, out_specs=P("rays", "depth", None), check_vma=False
    )
```

```python
import functools

import jax
import jax.numpy as jnp
from jax import lax
from jax.experimental import pallas as pl
from jax.experimental.pallas import tpu as pltpu
from jax.sharding import PartitionSpec as P

FEAT = 128
SAMPLES = 8
TH = 16
TW = 64
WIDE = 512
HEIGHT = 512
SLOTS = 5120
RAYS = 8192
LANES = 128
HALO = 4
PITCH = TW + 16
SMALL = pltpu.CompilerParams(vmem_limit_bytes=24 << 20)
PIECE = 1024
PACK = PIECE + 16
SUPER = 256
f32 = jnp.float32
bf16 = jnp.bfloat16
i32 = jnp.int32


def dot_nt(lhs, rhs):
    return lax.dot_general(lhs, rhs, (((1,), (1,)), ((), ())), preferred_element_type=f32)


def dot_nn(lhs, rhs):
    return jnp.dot(lhs, rhs, preferred_element_type=f32)


def iota(shape, axis):
    return lax.broadcasted_iota(i32, shape, axis)


def as_bf16(mask):
    return jnp.where(mask, 1.0, 0.0).astype(bf16)


def coordinates():
    place = lax.axis_index("depth")
    return place & 1, place >> 1, lax.axis_index("rays")


def rank_sum(parts):
    total = parts[0]
    for part in parts[1:]:
        total = total + part
    return jnp.sum(total, axis=0, keepdims=True)


def index_rays(pixel_ref, ids_ref, pos_ref, ray_ref):
    my_core, my_y, _ = coordinates()
    pixel = pixel_ref[...]
    row, col = pixel >> 9, pixel & (WIDE - 1)
    block_col = col >> 6
    core_rel = (block_col & 1) ^ my_core
    y_rel = ((block_col >> 1) - my_y) & 3
    group = core_rel * 128 + y_rel * 32 + (row >> 4)
    column = group.astype(f32).T.astype(i32)
    earlier = iota((LANES, LANES), 0) < iota((LANES, LANES), 1)
    iota16 = iota((16, LANES), 0)
    seen = jnp.zeros((16, 16), f32)
    ranks = []
    for j in range(RAYS // LANES):
        g = group[j : j + 1, :]
        same = jnp.where((column[:, j : j + 1] == g) & earlier, 1.0, 0.0)
        coarse = as_bf16(iota16 == (g >> 4))
        fine = iota16 == (g & 15)
        found = jnp.where(fine, dot_nn(seen.astype(bf16), coarse), 0.0)
        seen = seen + dot_nt(as_bf16(fine), coarse)
        parts = [same[8 * k : 8 * k + 8] for k in range(16)] + [found[:8], found[8:]]
        ranks.append(rank_sum(parts))
    rank = jnp.concatenate(ranks, axis=0).astype(i32)
    high = group >> 2
    low = (group & 3) * 32 + rank
    ray_ref[...] = high * LANES + low
    table = jnp.concatenate(
        [(high * LANES).astype(f32).T, low.astype(f32).T], axis=1
    ).astype(bf16)
    high_iota = iota((RAYS // LANES, LANES), 0)
    lane_iota = iota((LANES, LANES), 0)
    for j in range(SLOTS // LANES):
        ids = ids_ref[j : j + 1, :]
        hot = as_bf16(high_iota == (ids >> 7))
        found = dot_nn(table, jnp.concatenate([hot, hot], axis=0))
        found = jnp.where(lane_iota == (ids & (LANES - 1)), found, 0.0)
        pos_ref[j : j + 1, :] = rank_sum([found[8 * k : 8 * k + 8] for k in range(16)]).astype(i32)


def arrange_taps(k1_ref, k2_ref, main1, main2):
    for k_ref, main in ((k1_ref, main1), (k2_ref, main2)):
        for i in range(4):
            down, right = (i // 2) * 5 * FEAT, (i % 2) * FEAT
            main[down : down + 5 * FEAT, right : right + FEAT] = k_ref[i]


def info_kernel(pixel_ref, ray_ref, k1_ref, k2_ref, info_ref, main1, main2):
    arrange_taps(k1_ref, k2_ref, main1, main2)
    _, _, bundle = coordinates()
    pixel = pixel_ref[...]
    local_row = ((pixel >> 9) & (TH - 1)).astype(f32)
    local_col = (pixel & (TW - 1)).astype(f32)
    ray = ray_ref[...]
    lane_iota = iota((LANES, LANES), 0)
    iota8 = iota((8, LANES), 0)
    own = jnp.zeros((16, LANES), f32)
    for j in range(RAYS // LANES):
        at = ray[j : j + 1, :]
        mine = iota8 == (at >> 7)
        values = jnp.concatenate(
            [
                jnp.where(mine, local_row[j : j + 1, :], 0.0),
                jnp.where(mine, local_col[j : j + 1, :], 0.0),
            ],
            axis=0,
        ).astype(bf16)
        own = own + dot_nt(values, as_bf16(lane_iota == (at & (LANES - 1))))
    quarter = bundle & 3
    keep = (iota((16, LANES), 1) >> 5) == quarter
    for q in range(4):
        shift = ((quarter - q) & 3) * 32
        info_ref[q] = jnp.where(keep, pltpu.roll(own, shift, 1), 0.0)


def segment_kernel(
    live_smem,
    enc_hbm,
    gap_ref,
    pixel_ref,
    ids_ref,
    w1_ref,
    b1_ref,
    w2_ref,
    b2_ref,
    wd_ref,
    wf_ref,
    near_ref,
    far_ref,
    ray_ref,
    encoded,
    spread,
    hidden,
    first_a,
    first_b,
    wide1,
    wide2,
    pre,
    depth,
    colour_a,
    colour_b,
    table_ref,
    pos_ref,
    pos_smem,
    pos_sem,
    enc_sems,
):
    step = pl.program_id(0)
    rows = 2 * SUPER * SAMPLES

    def load(n):
        at = pl.ds(pl.multiple_of(n * rows, rows), rows)
        return pltpu.make_async_copy(enc_hbm.at[at], encoded.at[at], enc_sems.at[n])

    to_smem = pltpu.make_async_copy(pos_ref, pos_smem, pos_sem)
    half = SUPER * SAMPLES // 2

    @pl.when(step == 0)
    def _():
        for n in range(SLOTS // (2 * SUPER)):
            load(n).start()
        zero = jnp.zeros((FEAT, FEAT), bf16)
        for wide, w in ((wide1, w1_ref), (wide2, w2_ref)):
            wide[:FEAT, :FEAT] = w[0]
            wide[:FEAT, FEAT:] = zero
            wide[FEAT:, :FEAT] = zero
            wide[FEAT:, FEAT:] = w[0]
        index_rays(pixel_ref, ids_ref, pos_ref, ray_ref)
        to_smem.start()

    bias1 = jnp.concatenate([b1_ref[...]] * 2, axis=1)
    bias2 = jnp.concatenate([b2_ref[...]] * 2, axis=1)
    head = wd_ref[...].astype(f32)
    lane8 = iota((SAMPLES, LANES), 1)
    chunk = RAYS // (SLOTS // SUPER * 4) * 8 + 8
    start = pl.multiple_of(jnp.minimum(step * chunk, RAYS - chunk), 8)
    spread[pl.ds(start, chunk), :] = jnp.zeros((chunk, FEAT), f32)

    def layer_one(base, out):
        at = pl.multiple_of(step * rows + base, half)
        x = jnp.concatenate(
            [encoded[pl.ds(at, half), :], encoded[pl.ds(at + half, half), :]], axis=1
        )
        out[...] = jnp.maximum((dot_nn(x, wide1[...]) + bias1).astype(bf16), 0.0)

    def layer_two(source, block):
        h2 = jnp.maximum(dot_nn(source[...], wide2[...]) + bias2, 0.0)
        hidden[pl.ds(pl.multiple_of(block * half, half), half), :] = h2.astype(bf16)
        for side in range(2):
            part = h2[:, side * FEAT : (side + 1) * FEAT] * head
            total = jnp.sum(part, axis=1, keepdims=True)
            lined = jnp.zeros((SAMPLES, LANES), f32)
            for s in range(LANES):
                lined = jnp.where(lane8 == s, total[SAMPLES * s : SAMPLES * (s + 1), :], lined)
            pre[2 * block + side] = lined

    load(step).wait()
    layer_two(first_b, jnp.maximum(2 * step - 1, 0))
    layer_one(0, first_a)
    layer_two(first_a, 2 * step)
    layer_one(SUPER * SAMPLES, first_b)

    @pl.when(step == pl.num_programs(0) - 1)
    def _():
        live = live_smem[0]
        blocks = SLOTS // SUPER
        layer_two(first_b, blocks - 1)
        to_smem.wait()
        sample = iota((SAMPLES, LANES), 0)
        for b in range(SLOTS // LANES):
            v = pre[b]
            soft = jnp.maximum(v, 0.0) + jnp.log1p(jnp.exp(-jnp.abs(v)))
            opacity = soft * gap_ref[:, b * LANES : (b + 1) * LANES]
            inc = opacity
            for shift in (1, 2, 4):
                inc = inc + jnp.where(sample >= shift, pltpu.roll(inc, shift, 0), 0.0)
            weight = jnp.exp(opacity - inc) * (1.0 - jnp.exp(-opacity))
            alive = b * LANES + lane8 < live
            pre[b] = jnp.where(alive, weight, 0.0)
            depth[b : b + 1, :] = jnp.where(alive, inc, 0.0)[SAMPLES - 1 :, :]
        high_iota, low_iota = iota((RAYS // LANES, LANES), 0), iota((LANES, LANES), 0)

        def depth_table(block, table):
            for h in range(2):
                at = pos_ref[pl.ds(2 * block + h, 1), :]
                here = depth[pl.ds(2 * block + h, 1), :]
                coarse = here.astype(bf16).astype(f32)
                high = high_iota == (at >> 7)
                wanted = jnp.concatenate(
                    [jnp.where(high, coarse, 0.0), jnp.where(high, here - coarse, 0.0)], axis=0
                ).astype(bf16)
                table = table + dot_nt(wanted, as_bf16(low_iota == (at & (LANES - 1))))
            return table

        of_slot = iota((32, SUPER), 0) == (iota((32, SUPER), 1) >> 3)
        of_sample = as_bf16(iota((SAMPLES, SUPER), 0) == (iota((SAMPLES, SUPER), 1) & 7))

        def mix(block, colour):
            spaced = [
                lax.dot_general(
                    pre[2 * block + side].astype(bf16),
                    of_sample,
                    (((0,), (0,)), ((), ())),
                    preferred_element_type=f32,
                )
                for side in range(2)
            ]
            gathered = [None] * 8
            for i in range(4):
                rows = slice(32 * i, 32 * i + 32)
                both = jnp.concatenate(
                    [jnp.where(of_slot, spaced[side][rows], 0.0) for side in range(2)], axis=0
                ).astype(bf16)
                at = block * half + i * SUPER
                summed = dot_nn(both, hidden[pl.ds(at, SUPER), :])
                gathered[i] = summed[:32, :FEAT]
                gathered[i + 4] = summed[32:, FEAT:]
            mixed = jnp.concatenate(gathered, axis=0).astype(bf16)
            colour[...] = dot_nn(mixed, wf_ref[0])

        def scatter(block, colour):
            for s in range(SUPER):
                slot = block * SUPER + s
                at = pos_smem[slot // LANES, slot % LANES]
                spread[pl.ds(at, 1), :] = colour[s : s + 1, :]

        mix(0, colour_a)

        table_ref[...] = jnp.zeros_like(table_ref)
        for t in range(blocks // 2):

            @pl.when(live >= 0)
            def _(t=t):
                table = table_ref[...]
                mix(2 * t + 1, colour_b)
                scatter(2 * t, colour_a)
                table = depth_table(2 * t, table)
                if 2 * t + 2 < blocks:
                    mix(2 * t + 2, colour_a)
                scatter(2 * t + 1, colour_b)
                table_ref[...] = depth_table(2 * t + 1, table)

        table = table_ref[...]
        for n in range(8):
            k, g = 1 - n // 4, n % 4
            at = (4 * k + g) * PIECE
            out = (near_ref, far_ref)[k]
            out[g, :PIECE, :] = spread[at : at + PIECE, :].astype(bf16)
            rows = (4 * k + g) * 8
            out[g, PIECE:, :] = jnp.concatenate(
                [table[rows : rows + 8], table[64 + rows : 72 + rows]], axis=0
            ).astype(bf16)


def read_depth(ref):
    rows = ref[PIECE:, :].astype(f32)
    return rows[:8] + rows[8:]


def scaled(ref, factors, i):
    return ref[i * LANES : (i + 1) * LANES, :].astype(f32) * factors[:, i : i + 1]


def pair_kernel(mine, arrived, o0, o1, o2, o3):
    my_core, _, _ = coordinates()
    def combine(front_all, back_all):
        for g in range(4):
            front, back, out = front_all.at[g], back_all.at[g], (o0, o1, o2, o3)[g]
            d_front, d_back = read_depth(front), read_depth(back)
            fade = jnp.exp(-d_front).T
            for i in range(8):
                at = slice(i * LANES, (i + 1) * LANES)
                out[at, :] = (front[at, :].astype(f32) + scaled(back, fade, i)).astype(bf16)
            both = d_front + d_back
            coarse = both.astype(bf16).astype(f32)
            out[PIECE:, :] = jnp.concatenate([coarse, both - coarse], axis=0).astype(bf16)

    @pl.when(my_core == 0)
    def _():
        combine(mine, arrived)

    @pl.when(my_core == 1)
    def _():
        combine(arrived, mine)


def merge_kernel(p0_ref, p1_ref, p2_ref, p3_ref, info_ref, out_ref):
    _, y, _ = coordinates()
    pieces = (p0_ref, p1_ref, p2_ref, p3_ref)
    places = [(y - k) & 3 for k in range(4)]
    depths = [read_depth(ref) for ref in pieces]
    factors = []
    for a in range(4):
        before = jnp.zeros_like(depths[0])
        for b in range(4):
            if b != a:
                before = before + jnp.where(places[b] < places[a], depths[b], 0.0)
        factors.append(jnp.exp(-before).T)
    for i in range(8):
        total = scaled(pieces[0], factors[0], i)
        for k in range(1, 4):
            total = total + scaled(pieces[k], factors[k], i)
        total = total.astype(bf16)
        for q in range(4):
            tile = i * 4 + q
            out_ref[tile, :32, :] = total[q * 32 : q * 32 + 32, :]
            extra = jnp.concatenate(
                [
                    info_ref[q, i : i + 1, :],
                    info_ref[q, i + 8 : i + 9, :],
                    jnp.zeros((6, LANES), f32),
                ],
                axis=0,
            )
            out_ref[tile, 32:, :] = extra.astype(bf16)


def place_kernel(in_ref, out_ref, left_ref, right_ref):
    total = jnp.zeros((TH * TW, FEAT), f32)
    pixel_iota = iota((TH * TW, LANES), 0)
    for g in range(8):
        rows = jnp.concatenate([in_ref[4 * g + q, :32, :] for q in range(4)], axis=0)
        place = in_ref[4 * g, 32:, :].astype(f32)
        for q in range(1, 4):
            place = place + in_ref[4 * g + q, 32:, :].astype(f32)
        pixel = (place[0:1, :] * TW + place[1:2, :]).astype(i32)
        total = total + dot_nn(as_bf16(pixel_iota == pixel), rows)
    out_ref[...] = total.astype(bf16)
    left_ref[...] = jnp.concatenate([total[y * TW : y * TW + 8] for y in range(TH)]).astype(bf16)
    right_ref[...] = jnp.concatenate(
        [total[y * TW + TW - 8 : y * TW + TW] for y in range(TH)]
    ).astype(bf16)


def on_chip(array):
    return pltpu.with_memory_space_constraint(array, pltpu.VMEM)


def off_chip(array):
    return pltpu.with_memory_space_constraint(array, pltpu.HBM)


def whole(shape):
    return pl.BlockSpec(shape, lambda *_: (0,) * len(shape))


def shape_of(shape, dtype):
    return jax.ShapeDtypeStruct(shape, dtype)


VMEM = pl.BlockSpec(memory_space=pltpu.VMEM)


def segments(live, enc, gaps, pixel, ids, w1, b1, w2, b2, wd, wf):
    rows = 2 * SUPER * SAMPLES
    out = pltpu.VMEM((4, PACK, FEAT), bf16)
    return pl.pallas_call(
        segment_kernel,
        grid_spec=pltpu.PrefetchScalarGridSpec(
            num_scalar_prefetch=1,
            grid=(SLOTS * SAMPLES // rows,),
            in_specs=[pl.BlockSpec(memory_space=pltpu.HBM)]
            + [whole(a.shape) for a in (gaps, pixel, ids, w1, b1, w2, b2, wd, wf)],
            out_specs=[VMEM, VMEM, whole(pixel.shape)],
            scratch_shapes=[
                pltpu.VMEM((SLOTS * SAMPLES, FEAT), bf16),
                pltpu.VMEM((RAYS, FEAT), f32),
                pltpu.VMEM((SLOTS * SAMPLES // 2, 2 * FEAT), bf16),
                pltpu.VMEM((SUPER * SAMPLES // 2, 2 * FEAT), bf16),
                pltpu.VMEM((SUPER * SAMPLES // 2, 2 * FEAT), bf16),
                pltpu.VMEM((2 * FEAT, 2 * FEAT), bf16),
                pltpu.VMEM((2 * FEAT, 2 * FEAT), bf16),
                pltpu.VMEM((SLOTS // LANES, SAMPLES, LANES), f32),
                pltpu.VMEM((SLOTS // LANES, LANES), f32),
                pltpu.VMEM((SUPER, FEAT), f32),
                pltpu.VMEM((SUPER, FEAT), f32),
                pltpu.VMEM((2 * RAYS // LANES, LANES), f32),
                pltpu.VMEM((SLOTS // LANES, LANES), i32),
                pltpu.SMEM((SLOTS // LANES, LANES), i32),
                pltpu.SemaphoreType.DMA,
                pltpu.SemaphoreType.DMA((SLOTS // (2 * SUPER),)),
            ],
        ),
        out_shape=[out, out, shape_of(pixel.shape, i32)],
        compiler_params=pltpu.CompilerParams(vmem_limit_bytes=40 << 20),
        name="segments",
    )(live, *[off_chip(a) for a in (enc, gaps, pixel, ids, w1, b1, w2, b2, wd, wf)])


def exchanged(low, high, axis):
    size = lax.axis_size(axis)
    up = [(i, i + 1) for i in range(size - 1)]
    down = [(j, i) for i, j in up]
    return lax.ppermute(high, axis, up), lax.ppermute(low, axis, down)


def image_rows(block_ref, left_ref, right_ref, y):
    return [
        left_ref[8 * y : 8 * y + 8, :].astype(f32),
        block_ref[TW * y : TW * y + TW, :].astype(f32),
        right_ref[8 * y : 8 * y + 8, :].astype(f32),
    ]


def fill(rows, at, block_ref, left_ref, right_ref, first, last):
    for y in range(first, last):
        left, mid, right = image_rows(block_ref, left_ref, right_ref, y)
        base = at + (y - first) * PITCH
        rows[base : base + 8, :] = left
        rows[base + 8 : base + 8 + TW, :] = mid
        rows[base + 8 + TW : base + PITCH, :] = right


def conv_rows(source, at, first, count, main_ref, last, bias, shifted, partial, emit):
    total = (count + 4) * PITCH
    for j in range(5):
        shifted[:total, j * FEAT : (j + 1) * FEAT] = source[
            at + first + j : at + first + j + total, :
        ].astype(bf16)
    span = (count + 1) * PITCH
    parts = 1 if count == 4 else 5
    size = span // parts
    for p in range(parts):
        rows = slice(p * size, (p + 1) * size)
        below = slice(p * size + 2 * PITCH, (p + 1) * size + 2 * PITCH)
        partial[rows, :] = dot_nn(shifted[rows, :], main_ref[: 5 * FEAT, :]) + dot_nn(
            shifted[below, :], main_ref[5 * FEAT :, :]
        )
    for p in range(count // 4):
        base = p * 4 * PITCH
        rows = slice(base, base + 4 * PITCH)
        low = slice(base + PITCH, base + 5 * PITCH)
        end = slice(base + 4 * PITCH, base + 8 * PITCH)
        emit(
            p,
            partial[rows, :FEAT]
            + partial[low, FEAT:]
            + (dot_nn(shifted[end, :], last) + bias),
        )


def hidden_rows(value, first_row):
    flat = iota((4 * PITCH, FEAT), 0)
    col = lax.axis_index("depth") * TW - 2 + flat % PITCH
    row = lax.axis_index("rays") * TH + first_row + flat // PITCH
    inside = (row >= 0) & (row < HEIGHT) & (col >= 0) & (col < WIDE)
    return jnp.where(inside, jnp.maximum(value, 0.0), 0.0)


def inner_kernel(
    block_ref, left_ref, right_ref, main_ref, k_ref, b_ref, out_ref, rows, shifted, partial
):
    fill(rows, 0, block_ref, left_ref, right_ref, 0, TH)
    rows[TH * PITCH :, :] = jnp.zeros((16, FEAT), f32)

    def emit(p, value):
        out_ref[p * 4 * PITCH : (p + 1) * 4 * PITCH, :] = hidden_rows(value, 2 + 4 * p).astype(bf16)

    conv_rows(rows, 0, 4, 12, main_ref, k_ref[4], b_ref[...], shifted, partial, emit)


def outer_kernel(
    block_ref,
    left_ref,
    right_ref,
    above_ref,
    below_ref,
    inner_ref,
    main1_ref,
    k1_ref,
    b1_ref,
    main2_ref,
    k2_ref,
    b2_ref,
    out_ref,
    rows,
    hidden,
    shifted,
    partial,
):
    quad = 4 * PITCH
    rows[:quad, :] = above_ref[...].astype(f32)
    fill(rows, quad, block_ref, left_ref, right_ref, 0, 4)
    rows[2 * quad : 2 * quad + 16, :] = jnp.zeros((16, FEAT), f32)
    second = 2 * quad + 16
    fill(rows, second, block_ref, left_ref, right_ref, TH - 4, TH)
    rows[second + quad : second + 2 * quad, :] = below_ref[...].astype(f32)
    rows[second + 2 * quad :, :] = jnp.zeros((16, FEAT), f32)
    hidden[quad : 4 * quad, :] = inner_ref[...].astype(f32)
    hidden[5 * quad :, :] = jnp.zeros((16, FEAT), f32)
    for n, (at, first_row) in enumerate(((0, -2), (second, TH - 2))):

        def emit(p, value, n=n, first_row=first_row):
            hidden[4 * n * quad : (4 * n + 1) * quad, :] = hidden_rows(value, first_row)

        conv_rows(
            rows, at, 4, 4, main1_ref, k1_ref[4], b1_ref[...], shifted.at[n], partial.at[n], emit
        )

    def finish(p, value):
        value = value.astype(bf16)
        for y in range(4):
            out_ref[p * 4 + y] = value[y * PITCH : y * PITCH + TW, :]

    conv_rows(
        hidden, 0, 0, TH, main2_ref, k2_ref[4], b2_ref[...], shifted.at[2], partial.at[2], finish
    )


def on_device(
    encodings,
    spacing,
    ray_ids,
    live_count,
    pixel_of_ray,
    w_first,
    b_first,
    w_second,
    b_second,
    w_density,
    w_feature,
    kernel_one,
    bias_one,
    kernel_two,
    bias_two,
):
    pixel = pixel_of_ray.reshape(RAYS // LANES, LANES)
    near, far, ray = segments(
        live_count.reshape(1),
        encodings.reshape(SLOTS * SAMPLES, FEAT),
        spacing[0],
        pixel,
        ray_ids.reshape(SLOTS // LANES, LANES),
        w_first,
        b_first,
        w_second,
        b_second,
        w_density,
        w_feature,
    )
    arrived = lax.ppermute(far, "depth", [(i, i ^ 1) for i in range(8)])
    piece = pltpu.VMEM((PACK, FEAT), bf16)
    pieces = pl.pallas_call(
        pair_kernel,
        in_specs=[VMEM] * 2,
        out_specs=[VMEM] * 4,
        out_shape=[piece] * 4,
        compiler_params=SMALL,
        name="pair",
    )(near, on_chip(arrived))
    got = [
        lax.ppermute(pieces[k], "depth", [(i, (i + 2 * k) % 8) for i in range(8)])
        for k in range(1, 4)
    ]
    taps1, taps2 = kernel_one.reshape(5, 5 * FEAT, FEAT), kernel_two.reshape(5, 5 * FEAT, FEAT)
    main = pltpu.VMEM((10 * FEAT, 2 * FEAT), bf16)
    info, main1, main2 = pl.pallas_call(
        info_kernel,
        in_specs=[VMEM] * 4,
        out_specs=[VMEM] * 3,
        out_shape=[pltpu.VMEM((4, 16, LANES), f32), main, main],
        compiler_params=SMALL,
        name="info",
    )(pixel, ray, taps1, taps2)
    outgoing = pl.pallas_call(
        merge_kernel,
        in_specs=[VMEM] * 5,
        out_specs=VMEM,
        out_shape=pltpu.VMEM((32, 40, FEAT), bf16),
        compiler_params=SMALL,
        name="merge",
    )(pieces[0], *[on_chip(g) for g in got], info)
    incoming = lax.all_to_all(outgoing, "rays", split_axis=0, concat_axis=0, tiled=True)
    edge = shape_of((TH * 8, FEAT), bf16)
    block, low_edge, high_edge = pl.pallas_call(
        place_kernel,
        in_specs=[VMEM],
        out_specs=[VMEM] * 3,
        out_shape=[shape_of((TH * TW, FEAT), bf16), edge, edge],
        compiler_params=SMALL,
        name="place",
    )(on_chip(incoming))
    left, right = exchanged(low_edge, high_edge, "depth")
    parts = [left.reshape(TH, 8, FEAT), block.reshape(TH, TW, FEAT), right.reshape(TH, 8, FEAT)]
    first = jnp.concatenate([p[:HALO] for p in parts], axis=1).reshape(HALO * PITCH, FEAT)
    last = jnp.concatenate([p[TH - HALO :] for p in parts], axis=1).reshape(HALO * PITCH, FEAT)
    above, below = exchanged(first, last, "rays")
    above, below = on_chip(above), on_chip(below)
    left, right = on_chip(left), on_chip(right)
    inner = pl.pallas_call(
        inner_kernel,
        in_specs=[VMEM] * 6,
        out_specs=VMEM,
        out_shape=pltpu.VMEM((12 * PITCH, FEAT), bf16),
        scratch_shapes=[
            pltpu.VMEM((TH * PITCH + 16, FEAT), f32),
            pltpu.VMEM((TH * PITCH, 5 * FEAT), bf16),
            pltpu.VMEM((13 * PITCH, 2 * FEAT), f32),
        ],
        compiler_params=SMALL,
        name="inner",
    )(block, left, right, main1, taps1, bias_one[None])
    return pl.pallas_call(
        outer_kernel,
        in_specs=[VMEM] * 12,
        out_specs=VMEM,
        out_shape=shape_of((TH, TW, FEAT), bf16),
        scratch_shapes=[
            pltpu.VMEM((16 * PITCH + 32, FEAT), f32),
            pltpu.VMEM((20 * PITCH + 16, FEAT), f32),
            pltpu.VMEM((3, 20 * PITCH, 5 * FEAT), bf16),
            pltpu.VMEM((3, 17 * PITCH, 2 * FEAT), f32),
        ],
        compiler_params=SMALL,
        name="outer",
    )(
        block,
        left,
        right,
        above,
        below,
        inner,
        main1,
        taps1,
        bias_one[None],
        main2,
        taps2,
        bias_two[None],
    )


def solution(mesh):
    in_specs = (
        P("depth", "rays", None, None),
        P("depth", None, "rays"),
        P("depth", "rays"),
        P("depth", "rays"),
        P("rays"),
        P("depth", None, None),
        P("depth", None),
        P("depth", None, None),
        P("depth", None),
        P("depth", None),
        P("depth", None, None),
        P(),
        P(),
        P(),
        P(),
    )
    return jax.shard_map(
        on_device, mesh=mesh, in_specs=in_specs, out_specs=P("rays", "depth", None), check_vma=False
    )
```
